32 devices in a mesh: groups: 2 (over y), cell: 4 (over z), sc: 4 (over x, core).
Axes of the slice: x: 2, y: 2, z: 4, core: 2. Of those that a mesh axis runs over, the one named last changes fastest.
Arguments:
- symbols: bfloat16 [32, 2, 32, 4096], P(('groups', 'cell'), None, None, 'sc'), parts along dimension 0, may hold values from -4 to 4
- precoders: bfloat16 [32, 64, 16, 128], P(('groups', 'cell'), 'sc'), parts along dimension 0, may hold values from -1 to 1
- plan: int32 [32], P(('groups', 'cell')), parts along dimension 0, may hold values 0 or 1
- own_channel: bfloat16 [32, 16, 64, 128], P(('groups', 'cell'), None, 'sc'), parts along dimension 0, may hold values from -0.5 to 0.5
- cross_channel: bfloat16 [32, 16, 4, 64, 128], P(('groups', 'cell'), None, None, 'sc'), parts along dimension 0, may hold values from -0.375 to 0.375
- neighbours: int32 [32, 4], P(('groups', 'cell')), parts along dimension 0, may hold values from 0 to 15, as said below
- noise: bfloat16 [32, 16, 2, 2, 4096], P(('groups', 'cell'), None, None, None, 'sc'), parts along dimension 0, may hold values from -2 to 2
Outputs:
- time_signal: bfloat16 [32, 16, 2, 2, 4096], P(('groups', 'cell'), 'sc'), parts along dimension 0
The draws below stay inside these ranges and needn't reach their ends.
There are 2 independent parts, one for each index of `groups`. The reference program is written for one: setup_inputs(seed, part) draws one part's arguments, and reference() takes and returns one part's arrays. A program takes and returns all parts, laid end to end along the dimension named above; each array names one. Nothing has to cross between parts.
Inputs may be any that keep to these rules, and one draw needn't show every extreme that they name: `neighbours`: each cell's 4 entries are distinct cells other than itself, each within 4 cells of it along the cycle of all 16 cells, where cell 0 follows cell 16 - 1.
All inputs are finite; a program needn't handle non-finite values. No bound on the sum of `plan` on one device may be relied on, other than what follows from the above.
Results may differ from the reference program's by a relative error of at most 0.0057.
Values may be sent and summed in bfloat16 or wider, within the bound.
No kernel may reach another device: no remote copies, remote signals or barrier semaphores. Data moves between devices by JAX's collectives and lax.ppermute only.
A program may use at most 64 MiB of HBM per device.

```python
import math
import jax
import jax.numpy as jnp
from jax import lax

A = 64
U = 16
K = 4
SYMS = 2
NT = 4096
CELL_DEV = 4
CELLS = 16
NSB = 64


def draw_neighbours(key, part):
    reach_cells = CELL_DEV
    scores = jax.random.randint(key, (CELLS, 2 * reach_cells), 0, 1 << 20)
    scores = scores * (2 * reach_cells) + jnp.arange(2 * reach_cells, dtype=jnp.int32)[None, :]
    ranked = jnp.argsort(scores, axis=1, stable=True)[:, :K].astype(jnp.int32)
    offsets = jnp.where(ranked < reach_cells, ranked - reach_cells, ranked - reach_cells + 1)
    cell_ids = jnp.arange(CELLS, dtype=jnp.int32)[:, None]
    return ((cell_ids + offsets) % CELLS).astype(jnp.int32)


def plant(array, stream_key, least, high):
    extent = array.shape
    index_at = [jax.random.randint(jax.random.fold_in(stream_key, axis), (), 0, extent[axis]) for axis in range(len(extent))]
    array = array.at[tuple(index_at)].set(least)
    longest = extent.index(max(extent))
    index_at[longest] = (index_at[longest] + 1) % extent[longest]
    return array.at[tuple(index_at)].set(high)


def block_scale(stream_key, dims, split, low, high):
    gain = 1.0
    for axis_at, blocks in split:
        draws = jax.random.uniform(jax.random.fold_in(jax.random.fold_in(stream_key, 6), axis_at), (blocks,), jnp.float32, low / len(split), high / len(split))
        gain = gain * jnp.repeat(jnp.exp(draws), dims[axis_at] // blocks).reshape((-1,) + (1,) * (len(dims) - 1 - axis_at))
    return gain


def scatter_about(key, extent, scale, bound, pieces=(), held_as=jnp.bfloat16):
    values = scale * jax.random.normal(key, extent, jnp.float32)
    if pieces:
        values = values * block_scale(key, extent, pieces, -0.22, 0.18)
    return jnp.clip(values, -bound, bound).astype(held_as)


def setup_inputs(seed: int = 0, part: int = 0) -> dict:
    splits = jax.random.split(jax.random.key(seed), 8)
    own_keys = jax.random.split(jax.random.fold_in(splits[7], part), 8)
    symbols = scatter_about(own_keys[0], (CELLS, SYMS, 2 * U, NT), 1.0, 4.0, ((0, 4), (3, 4)))
    precoders = scatter_about(own_keys[1], (CELLS, NSB, U, 2 * A), (2 * U) ** -0.5, 1.0, ((0, 4), (1, 4)))
    plan = plant((jax.random.randint(own_keys[2], (CELLS,), 0, 4) < 3).astype(jnp.int32), jax.random.fold_in(own_keys[2], 1), 0, 1)
    own_channel = scatter_about(own_keys[3], (CELLS, U, NSB, 2 * A), (2 * A) ** -0.5, 0.5, ((0, 4), (2, 4)))
    cross_channel = scatter_about(own_keys[4], (CELLS, U, K, NSB, 2 * A), (4 * A) ** -0.5, 0.375, ((0, 4), (3, 4)))
    neighbours = draw_neighbours(jax.random.fold_in(jax.random.fold_in(splits[7], part), 71), part)
    noise = scatter_about(own_keys[6], (CELLS, U, SYMS, 2, NT), 0.3, 2.0, ((0, 4), (4, 4)))
    return dict(symbols=symbols, precoders=precoders, plan=plan, own_channel=own_channel, cross_channel=cross_channel, neighbours=neighbours, noise=noise)


def precode_cell(weights, data_streams):
    half = weights.shape[-1] // 2
    real_part = weights[..., :half].astype(jnp.float32)
    imag_part = weights[..., half:].astype(jnp.float32)
    upper = jnp.concatenate([real_part, imag_part], axis=-1)
    lower = jnp.concatenate([-imag_part, real_part], axis=-1)
    blocks = jnp.concatenate([upper, lower], axis=-2)
    symbol_total, spatial_layer_count, subcarrier_total = data_streams.shape
    subband_total = weights.shape[0]
    grouped_values = data_streams.astype(jnp.float32).reshape(symbol_total, spatial_layer_count, subband_total, subcarrier_total // subband_total)
    output_values = jnp.einsum('tvbs,bva->tbsa', grouped_values, blocks, precision=lax.Precision.HIGHEST)
    return output_values.reshape(symbol_total, subcarrier_total, -1).astype(jnp.bfloat16)

def receive_cell(transmit_signal, channel_matrix):
    half = channel_matrix.shape[-1] // 2
    real_part = channel_matrix[..., :half].astype(jnp.float32)
    imag_part = channel_matrix[..., half:].astype(jnp.float32)
    to_real = jnp.concatenate([real_part, -imag_part], axis=-1)
    to_imag = jnp.concatenate([imag_part, real_part], axis=-1)
    blocks = jnp.stack([to_real, to_imag], axis=-1)
    symbol_total, subcarrier_total, spatial_layers = transmit_signal.shape
    subband_total = channel_matrix.shape[1]
    grouped_values = transmit_signal.astype(jnp.float32).reshape(symbol_total, subband_total, subcarrier_total // subband_total, spatial_layers)
    output_values = jnp.einsum('tbsa,ubaz->utzbs', grouped_values, blocks, precision=lax.Precision.HIGHEST)
    return output_values.reshape(channel_matrix.shape[0], symbol_total, 2, subcarrier_total)

def reference(symbols, precoders, plan, own_channel, cross_channel, neighbours, noise):

    def cell_signal(cell_id):
        gated_symbols = symbols[cell_id] * plan[cell_id].astype(jnp.bfloat16)
        return precode_cell(precoders[cell_id], gated_symbols)

    def one_cell(cell_id):
        received = receive_cell(cell_signal(cell_id), own_channel[cell_id])
        for slot_index in range(K):
            source = cell_signal(neighbours[cell_id, slot_index])
            received = received + receive_cell(source, cross_channel[cell_id, :, slot_index])
        freq_grid = (received + noise[cell_id].astype(jnp.float32)).astype(jnp.bfloat16).astype(jnp.float32)
        complex_grid = freq_grid[:, :, 0, :] + 1j * freq_grid[:, :, 1, :]
        timed = jnp.fft.ifft(complex_grid, axis=-1) * math.sqrt(NT)
        return jnp.stack([jnp.real(timed), jnp.imag(timed)], axis=2).astype(jnp.bfloat16)
    return lax.map(one_cell, jnp.arange(CELLS, dtype=jnp.int32))
```

```python
import functools
import math

import jax
import jax.numpy as jnp
import numpy as np
from jax import lax
from jax.experimental import pallas as pl
from jax.experimental.pallas import tpu as pltpu
from jax.sharding import PartitionSpec as P

LANES = 128
SMEM = pltpu.MemorySpace.SMEM
BF16, F32 = jnp.bfloat16, jnp.float32
NT = (((1,), (1,)), ((), ()))


def combined_channel(idx_ref, h, p, base, slots, cells, users):
    half = p.shape[-1] // 2
    wide = p.astype(F32)
    lane = lax.broadcasted_iota(jnp.int32, wide.shape[1:], 1)
    p0 = [jnp.where(lane < half, wide[n], -wide[n]) for n in range(cells)]
    p1 = [pltpu.roll(wide[n], half, 1) for n in range(cells)]
    rows = [r for n in range(cells) for r in (p0[n], -p1[n])] + [r for n in range(cells) for r in (p1[n], p0[n])]
    rhs = jnp.concatenate(rows, axis=0).astype(BF16)
    prod = lax.dot_general(h, rhs, NT, preferred_element_type=F32)
    width = prod.shape[1] // 2
    source = lax.broadcasted_iota(jnp.int32, (users, width), 1) // (width // cells)
    out = []
    for z in range(2):
        for c in range(cells):
            acc = jnp.zeros((users, width), F32)
            for k in range(slots):
                start = (k * cells + c) * users
                part = prod[start : start + users, z * width : (z + 1) * width]
                acc = jnp.where(source == idx_ref[c, k] - base, part, acc)
            out.append(acc)
    return jnp.concatenate(out, axis=0).astype(BF16)


def pick_subbands(res, per):
    rows = res.shape[0] // per
    lane = lax.broadcasted_iota(jnp.int32, (rows, LANES), 1) // (LANES // per)
    out = res[:rows]
    for i in range(1, per):
        out = jnp.where(lane == i, res[i * rows : (i + 1) * rows], out)
    return out


def own_kernel(slots, cells, users, idx_ref, h_ref, p_ref, s_ref, noise_ref, acc_ref):
    per = h_ref.shape[0]
    g = jnp.concatenate(
        [combined_channel(idx_ref, h_ref[i], p_ref[:, i], cells, slots, cells, users) for i in range(per)], axis=0
    )
    for t in range(acc_ref.shape[0]):
        res = jnp.dot(g, s_ref[t], preferred_element_type=F32)
        acc_ref[t, 0] = noise_ref[t, 0].astype(F32) + pick_subbands(res, per)


def remote_kernel(slots, cells, users, idx_ref, h_ref, a_ref, b_ref, g_ref):
    per = h_ref.shape[0]
    out = []
    for i in range(per):
        parts = [
            combined_channel(idx_ref, h_ref[i], ref[:, i], base, slots, cells, users)
            for ref, base in ((a_ref, 0), (b_ref, 2 * cells))
        ]
        out.append(jnp.concatenate(parts, axis=1))
    g_ref[0] = jnp.concatenate(out, axis=0)


def grid_kernel(per, cells, users, me_ref, g_ref, a_ref, b_ref, acc_ref, *refs):
    outs, y, tiles = refs[:-2], refs[-2], refs[-1]
    blocks, rows = acc_ref.shape[0], acc_ref.shape[1]
    for r in range(blocks):
        lanes = slice(r * LANES, (r + 1) * LANES)
        s = jnp.concatenate([a_ref[:, lanes], b_ref[:, lanes]], axis=0)
        res = jnp.dot(g_ref[r], s, preferred_element_type=F32)
        y[r * rows : (r + 1) * rows] = acc_ref[r] + pick_subbands(res, per)
    half = rows // 2
    for row in range(half):
        tile = [y[pl.ds(z * half + row, blocks, stride=rows), :] for z in range(2)]
        tiles[row % users, row // users] = jnp.concatenate(tile, axis=0).astype(BF16)
    count = len(outs)
    for d in range(count):
        group = lax.rem(me_ref[0] + d, count)
        outs[d][...] = tiles[pl.ds(group * (users // count), users // count)]


def time_kernel(me_ref, w1_ref, tw_ref, w2_ref, *refs):
    parts, out_ref = refs[:-1], refs[-1]
    seqs = parts[0].shape[0] * parts[0].shape[1]
    rows = tw_ref.shape[1]
    w1 = w1_ref[me_ref[0]]
    w2 = w2_ref[...]
    n2 = w2.shape[0] // 2
    per = LANES // rows
    batch = min(seqs, 2 * per)
    cells = parts[0].shape[1]
    for first in range(0, seqs, batch):
        data = jnp.concatenate(
            [jnp.concatenate([p[q // cells, q % cells] for p in parts], axis=0) for q in range(first, first + batch)], axis=1
        )
        both = jnp.dot(w1, data, preferred_element_type=F32)
        both = both[: 2 * rows] + both[2 * rows :]
        turned = []
        for q in range(batch):
            re = both[:rows, q * LANES : (q + 1) * LANES]
            im = both[rows:, q * LANES : (q + 1) * LANES]
            turned.append(
                jnp.concatenate([re * tw_ref[0] - im * tw_ref[1], re * tw_ref[1] + im * tw_ref[0]], axis=1)
            )
        turned = jnp.concatenate(turned, axis=0)
        high = turned.astype(BF16)
        low = (turned - high.astype(F32)).astype(BF16)
        prod = lax.dot_general(w2, high, NT, preferred_element_type=F32)
        prod = prod[:n2] + prod[n2:] + lax.dot_general(w2[:n2], low, NT, preferred_element_type=F32)
        for z in range(2):
            for q in range(batch):
                group, at = divmod(q, per)
                pieces = []
                for i in range(per):
                    top = z * LANES + i * rows
                    left = group * LANES + at * rows
                    pieces.append(prod[top : top + rows, left : left + rows])
                seq = first + q
                out_ref[seq % cells, seq // cells, z] = jnp.concatenate(pieces, axis=1).astype(BF16)


def rotation(angle):
    return np.block([[np.cos(angle), -np.sin(angle)], [np.sin(angle), np.cos(angle)]])


def split_rows(table):
    high = table.astype(jnp.bfloat16)
    low = (table - high.astype(np.float64)).astype(jnp.bfloat16)
    return np.concatenate([high, low], axis=0)


def tables(length, parts):
    rows = length // LANES
    local = rows // parts
    m = np.arange(rows)
    w1 = []
    for me in range(parts):
        order = np.concatenate([(me - d) % parts * local + np.arange(local) for d in range(parts)])
        angle = 2 * np.pi * (np.outer(m, order) % rows) / rows
        full = rotation(angle).reshape(2 * rows, 2, parts, local).transpose(0, 2, 1, 3).reshape(2 * rows, 2 * rows)
        w1.append(split_rows(full))
    lane = np.arange(LANES)
    angle = 2 * np.pi * (np.outer(m, lane) % length) / length
    twist = (np.stack([np.cos(angle), np.sin(angle)]) / math.sqrt(length)).astype(np.float32)
    per = LANES // rows
    order = np.arange(LANES).reshape(rows, per).T.reshape(-1)
    angle = 2 * np.pi * (np.outer(order, lane) % LANES) / LANES
    w2 = split_rows(rotation(angle))
    return np.stack(w1), twist, w2


def whole(shape):
    return pl.BlockSpec(shape, lambda *_: (0,) * len(shape))


def body(symbols, precoders, plan, own_channel, cross_channel, neighbours, noise):
    cells, times, streams, width = symbols.shape
    subbands, users, slots, ants = precoders.shape[1], own_channel.shape[1], cross_channel.shape[2], precoders.shape[3]
    blocks = width // LANES
    per = subbands // blocks
    parts = lax.axis_size("sc")
    ring = lax.axis_size("cell")
    length = width * parts
    rows = 2 * cells * users
    up = [(i, (i + 1) % ring) for i in range(ring)]
    down = [(j, i) for i, j in up]

    def both_ways(x):
        return lax.ppermute(x, "cell", up), lax.ppermute(x, "cell", down)

    p_before, p_after = both_ways(precoders)
    gated = symbols * plan.astype(BF16)[:, None, None, None]
    gated = gated.transpose(1, 0, 2, 3).reshape(times, cells * streams, width)
    halos = [both_ways(gated[t]) for t in range(times)]

    base = lax.axis_index("cell") * cells
    idx = (neighbours - base + cells) % (cells * ring)
    idx = jnp.concatenate([idx, cells + jnp.arange(cells, dtype=jnp.int32)[:, None]], axis=1)
    cross = cross_channel.transpose(3, 2, 0, 1, 4).reshape(subbands, slots * cells * users, ants)
    own = own_channel.transpose(2, 0, 1, 3).reshape(subbands, cells * users, ants)
    chan = jnp.concatenate([cross, own], axis=1)
    noise_rows = noise.reshape(cells, users, times, 2, blocks, LANES).transpose(2, 4, 3, 0, 1, 5)
    noise_rows = noise_rows.reshape(times, blocks, rows, LANES)
    me = lax.axis_index("sc").astype(jnp.int32)[None]

    smem = pl.BlockSpec(memory_space=SMEM)
    p_spec = pl.BlockSpec((cells, per) + precoders.shape[2:], lambda r: (0, r, 0, 0))
    acc = pl.pallas_call(
        functools.partial(own_kernel, slots + 1, cells, users),
        grid=(blocks,),
        in_specs=[
            smem,
            pl.BlockSpec((per, (slots + 1) * cells * users, ants), lambda r: (r, 0, 0)),
            p_spec,
            pl.BlockSpec((times, cells * streams, LANES), lambda r: (0, 0, r)),
            pl.BlockSpec((times, 1, rows, LANES), lambda r: (0, r, 0, 0)),
        ],
        out_specs=pl.BlockSpec((times, 1, rows, LANES), lambda r: (0, r, 0, 0)),
        out_shape=jax.ShapeDtypeStruct((times, blocks, rows, LANES), F32),
        name="own_cells",
        cost_estimate=pl.CostEstimate(flops=2_000_000_000, bytes_accessed=4_000_000, transcendentals=0),
    )(idx, chan, precoders, gated, noise_rows)
    comb = pl.pallas_call(
        functools.partial(remote_kernel, slots, cells, users),
        grid=(blocks,),
        in_specs=[smem, pl.BlockSpec((per, slots * cells * users, ants), lambda r: (r, 0, 0)), p_spec, p_spec],
        out_specs=pl.BlockSpec((1, per * rows, 2 * cells * streams), lambda r: (r, 0, 0)),
        out_shape=jax.ShapeDtypeStruct((blocks, per * rows, 2 * cells * streams), BF16),
        name="other_cells",
        cost_estimate=pl.CostEstimate(flops=2_000_000_000, bytes_accessed=4_000_000, transcendentals=0),
    )(idx, chan, p_before, p_after)

    w1, twist, w2 = (jnp.asarray(x) for x in tables(length, parts))
    share = users // parts
    done = []
    for t in range(times):
        tile = (share, cells, 2 * blocks, LANES)
        sent = pl.pallas_call(
            functools.partial(grid_kernel, per, cells, users),
            in_specs=[smem] + [whole(x.shape) for x in (comb, *halos[t], acc[t])],
            out_specs=[whole(tile)] * parts,
            out_shape=[jax.ShapeDtypeStruct(tile, BF16)] * parts,
            grid=(1,),
            scratch_shapes=[
                pltpu.VMEM((blocks * rows, LANES), F32),
                pltpu.VMEM((users, cells, 2 * blocks, LANES), BF16),
            ],
            name="grid",
            cost_estimate=pl.CostEstimate(flops=1_000_000_000, bytes_accessed=3_000_000, transcendentals=0),
        )(me, comb, *halos[t], acc[t])
        got = [
            lax.ppermute(sent[d], "sc", [(i, (i + d) % parts) for i in range(parts)]) if d else sent[0] for d in range(parts)
        ]
        shape = (cells, share, 2, length // LANES, LANES)
        done.append(
            pl.pallas_call(
                time_kernel,
                in_specs=[smem] + [whole(x.shape) for x in (w1, twist, w2, *got)],
                out_specs=whole(shape),
                out_shape=jax.ShapeDtypeStruct(shape, BF16),
                grid=(1,),
                name="time",
                cost_estimate=pl.CostEstimate(flops=1_000_000_000, bytes_accessed=2_000_000, transcendentals=0),
            )(me, w1, twist, w2, *got)
        )
    return jnp.stack(done, axis=2).reshape(cells, share, times, 2, length)


def solution(mesh):
    in_specs = (
        P(("groups", "cell"), None, None, "sc"),
        P(("groups", "cell"), "sc", None, None),
        P(("groups", "cell")),
        P(("groups", "cell"), None, "sc", None),
        P(("groups", "cell"), None, None, "sc", None),
        P(("groups", "cell"), None),
        P(("groups", "cell"), None, None, None, "sc"),
    )
    out_specs = P(("groups", "cell"), "sc", None, None, None)
    return jax.shard_map(body, mesh=mesh, in_specs=in_specs, out_specs=out_specs, check_vma=False)
```

```python
import functools
import math

import jax
import jax.numpy as jnp
import numpy as np
from jax import lax
from jax.experimental import pallas as pl
from jax.experimental.pallas import tpu as pltpu
from jax.sharding import PartitionSpec as P

LANES = 128
SMEM = pltpu.MemorySpace.SMEM
BF16, F32 = jnp.bfloat16, jnp.float32
NT = (((1,), (1,)), ((), ()))


def gate_kernel(plan_ref, x_ref, *outs):
    cells, times, streams, _ = x_ref.shape
    for c in range(cells):
        on = plan_ref[c] != 0
        for t in range(times):
            x = x_ref[c, t]
            outs[t][c * streams : (c + 1) * streams] = jnp.where(on, x, jnp.zeros_like(x))


def place(near_ref, base_ref, total, cells, slots):
    table = []
    for c in range(cells):
        row = []
        for k in range(slots):
            at = near_ref[c, k] - base_ref[0] + cells
            at = jnp.where(at < 0, at + total, at)
            row.append(jnp.where(at >= total, at - total, at))
        table.append(row)
    return table


def combined_channel(masks, h, p):
    cells = p.shape[0]
    slots = len(masks[0])
    users = h.shape[0] // (slots * cells)
    half = p.shape[-1] // 2
    wide = p.astype(F32)
    lane = lax.broadcasted_iota(jnp.int32, wide.shape[1:], 1)
    p0 = [jnp.where(lane < half, wide[n], -wide[n]) for n in range(cells)]
    p1 = [pltpu.roll(wide[n], half, 1) for n in range(cells)]
    rows = [r for n in range(cells) for r in (p0[n], -p1[n])] + [r for n in range(cells) for r in (p1[n], p0[n])]
    rhs = jnp.concatenate(rows, axis=0).astype(BF16)
    prod = lax.dot_general(h, rhs, NT, preferred_element_type=F32)
    width = prod.shape[1] // 2
    out = []
    for z in range(2):
        for c in range(cells):
            acc = jnp.zeros((users, width), F32)
            for k in range(slots):
                start = (k * cells + c) * users
                part = prod[start : start + users, z * width : (z + 1) * width]
                acc = jnp.where(masks[c][k], part, acc)
            out.append(acc)
    return jnp.concatenate(out, axis=0).astype(BF16)


def source_masks(table, base, users, cells, width):
    source = lax.broadcasted_iota(jnp.int32, (users, width), 1) // (width // cells) + base
    return [[source == at for at in row] for row in table]


def pick_subbands(res, per):
    rows = res.shape[0] // per
    lane = lax.broadcasted_iota(jnp.int32, (rows, LANES), 1) // (LANES // per)
    out = res[:rows]
    for i in range(1, per):
        out = jnp.where(lane == i, res[i * rows : (i + 1) * rows], out)
    return out


def own_kernel(total, near_ref, base_ref, h_ref, own_ref, p_ref, *refs):
    times = len(refs) // 2
    s_refs, acc_refs = refs[:times], refs[times:]
    blocks, rows, _ = acc_refs[0].shape
    subbands, cells = p_ref.shape[1], p_ref.shape[0]
    per = subbands // blocks
    users = own_ref.shape[1] // cells
    table = place(near_ref, base_ref, total, cells, h_ref.shape[1] // (cells * users))
    table = [row + [cells + c] for c, row in enumerate(table)]
    masks = source_masks(table, cells, users, cells, s_refs[0].shape[0])
    for r in range(blocks):
        g = []
        for b in range(r * per, (r + 1) * per):
            h = jnp.concatenate([h_ref[b], own_ref[b]], axis=0)
            g.append(combined_channel(masks, h, p_ref[:, b]))
        g = jnp.concatenate(g, axis=0)
        for t in range(times):
            res = jnp.dot(g, s_refs[t][:, r * LANES : (r + 1) * LANES], preferred_element_type=F32)
            acc_refs[t][r] = pick_subbands(res, per)


def remote_kernel(total, users, near_ref, base_ref, h_ref, a_ref, b_ref, g_ref):
    subbands, cells = a_ref.shape[1], a_ref.shape[0]
    blocks = g_ref.shape[0]
    per = subbands // blocks
    width = g_ref.shape[2] // 2
    rows = 2 * cells * users
    table = place(near_ref, base_ref, total, cells, h_ref.shape[1] // (cells * users))
    for side, (ref, base) in enumerate(((a_ref, 0), (b_ref, 2 * cells))):
        masks = source_masks(table, base, users, cells, width)
        for b in range(subbands):
            r, i = divmod(b, per)
            g_ref[r, i * rows : (i + 1) * rows, side * width : (side + 1) * width] = combined_channel(
                masks, h_ref[b], ref[:, b]
            )


def grid_kernel(t, me_ref, g_ref, a_ref, b_ref, acc_ref, noise_ref, *refs):
    outs, y, tiles = refs[:-2], refs[-2], refs[-1]
    blocks, rows, _ = acc_ref.shape
    per = g_ref.shape[1] // rows
    cells, users = noise_ref.shape[:2]
    for r in range(blocks):
        lanes = slice(r * LANES, (r + 1) * LANES)
        s = jnp.concatenate([a_ref[:, lanes], b_ref[:, lanes]], axis=0)
        res = jnp.dot(g_ref[r], s, preferred_element_type=F32)
        y[r * rows : (r + 1) * rows] = acc_ref[r] + pick_subbands(res, per)
    half = rows // 2
    for row in range(half):
        c, u = divmod(row, users)
        tile = y[pl.ds(row, 2 * blocks, stride=half), :] + noise_ref[c, u, t].astype(F32)
        tiles[u, c] = tile.astype(BF16)
    count = len(outs)
    for d in range(count):
        group = lax.rem(me_ref[0] + d, count)
        outs[d][...] = tiles[pl.ds(group * (users // count), users // count)]


def time_kernel(t, me_ref, w1_ref, tw_ref, w2_ref, *refs):
    parts, out_ref = refs[: w1_ref.shape[0]], refs[-1]
    share, cells = parts[0].shape[:2]
    seqs = share * cells
    rows = tw_ref.shape[1]
    w1 = w1_ref[me_ref[0]]
    w2 = w2_ref[...]
    n2 = w2.shape[0] // 2
    per = LANES // rows
    batch = min(seqs, 2 * per)
    for first in range(0, seqs, batch):
        data = jnp.concatenate(
            [jnp.concatenate([p[q // cells, q % cells] for p in parts], axis=0) for q in range(first, first + batch)], axis=1
        )
        both = jnp.dot(w1, data, preferred_element_type=F32)
        both = both[: 2 * rows] + both[2 * rows :]
        turned = []
        for q in range(batch):
            re = both[:rows, q * LANES : (q + 1) * LANES]
            im = both[rows:, q * LANES : (q + 1) * LANES]
            turned.append(
                jnp.concatenate([re * tw_ref[0] - im * tw_ref[1], re * tw_ref[1] + im * tw_ref[0]], axis=1)
            )
        turned = jnp.concatenate(turned, axis=0)
        high = turned.astype(BF16)
        low = (turned - high.astype(F32)).astype(BF16)
        prod = lax.dot_general(w2, high, NT, preferred_element_type=F32)
        prod = prod[:n2] + prod[n2:] + lax.dot_general(w2[:n2], low, NT, preferred_element_type=F32)
        tall = n2 // per
        for q in range(batch):
            group, at = divmod(q, per)
            left = group * LANES + at * rows
            pieces = [prod[i * tall : (i + 1) * tall, left : left + rows] for i in range(per)]
            seq = first + q
            out_ref[seq % cells, seq // cells, 0] = jnp.concatenate(pieces, axis=1).astype(BF16)


def rotation(angle):
    return np.block([[np.cos(angle), -np.sin(angle)], [np.sin(angle), np.cos(angle)]])


def split_rows(table):
    high = table.astype(jnp.bfloat16)
    low = (table - high.astype(np.float64)).astype(jnp.bfloat16)
    return np.concatenate([high, low], axis=0)


def tables(length, parts):
    rows = length // LANES
    local = rows // parts
    m = np.arange(rows)
    w1 = []
    for me in range(parts):
        order = np.concatenate([(me - d) % parts * local + np.arange(local) for d in range(parts)])
        angle = 2 * np.pi * (np.outer(m, order) % rows) / rows
        full = rotation(angle).reshape(2 * rows, 2, rows).transpose(0, 2, 1).reshape(2 * rows, 2 * rows)
        w1.append(split_rows(full))
    lane = np.arange(LANES)
    angle = 2 * np.pi * (np.outer(m, lane) % length) / length
    twist = (np.stack([np.cos(angle), np.sin(angle)]) / math.sqrt(length)).astype(np.float32)
    per = LANES // rows
    angle = 2 * np.pi * (np.outer(lane, lane) % LANES) / LANES
    w2 = rotation(angle).reshape(2, rows, per, 2 * LANES).transpose(2, 1, 0, 3).reshape(2 * LANES, 2 * LANES)
    return np.stack(w1), twist, split_rows(w2)


def whole(shape):
    return pl.BlockSpec(shape, lambda *_: (0,) * len(shape))


def body(symbols, precoders, plan, own_channel, cross_channel, neighbours, noise):
    cells, times, streams, width = symbols.shape
    subbands, users, slots, ants = precoders.shape[1], own_channel.shape[1], cross_channel.shape[2], precoders.shape[3]
    blocks = width // LANES
    per = subbands // blocks
    parts = lax.axis_size("sc")
    ring = lax.axis_size("cell")
    length = width * parts
    rows = 2 * cells * users
    up = [(i, (i + 1) % ring) for i in range(ring)]
    down = [(j, i) for i, j in up]

    def both_ways(x):
        return lax.ppermute(x, "cell", up), lax.ppermute(x, "cell", down)

    total = cells * ring
    tall = cells * streams
    vmem = pl.BlockSpec(memory_space=pltpu.MemorySpace.VMEM)
    smem = pl.BlockSpec(memory_space=SMEM)

    def call(kernel, name, out_shape, ins, scalars, scratch=(), grant=16, flops=1_000_000_000, **more):
        return pl.pallas_call(
            kernel,
            in_specs=[smem] * scalars + [vmem] * (len(ins) - scalars),
            out_specs=jax.tree.map(lambda _: vmem, out_shape),
            out_shape=out_shape,
            scratch_shapes=scratch,
            name=name,
            compiler_params=pltpu.CompilerParams(vmem_limit_bytes=grant << 20),
            cost_estimate=pl.CostEstimate(flops=flops, bytes_accessed=4_000_000, transcendentals=0),
        )(*ins)

    p_before, p_after = both_ways(precoders)
    gated = call(gate_kernel, "gate", [jax.ShapeDtypeStruct((tall, width), BF16)] * times, (plan, symbols), 1)
    halos = [both_ways(g) for g in gated]

    base = (lax.axis_index("cell") * cells).astype(jnp.int32)[None]
    me = lax.axis_index("sc").astype(jnp.int32)[None]
    cross = cross_channel.transpose(3, 2, 0, 1, 4).reshape(subbands, slots * cells * users, ants)
    own = own_channel.transpose(2, 0, 1, 3).reshape(subbands, cells * users, ants)
    noise_tiles = noise.reshape(cells, users, times, 2, blocks, LANES).transpose(0, 1, 2, 4, 3, 5)
    noise_tiles = noise_tiles.reshape(cells, users, times, 2 * blocks, LANES)

    acc = call(
        functools.partial(own_kernel, total), "own_cells", [jax.ShapeDtypeStruct((blocks, rows, LANES), F32)] * times,
        (neighbours, base, cross, own, precoders, *gated), 2,
    )
    comb = call(
        functools.partial(remote_kernel, total, users), "other_cells",
        jax.ShapeDtypeStruct((blocks, per * rows, 2 * tall), BF16),
        (neighbours, base, cross, p_before, p_after), 2,
    )

    w1, twist, w2 = (jnp.asarray(x) for x in tables(length, parts))
    share = users // parts
    full = (cells, share, times, 2 * length // LANES, LANES)
    out = None
    for t in range(times):
        tile = (share, cells, 2 * blocks, LANES)
        sent = call(
            functools.partial(grid_kernel, t), "grid", [jax.ShapeDtypeStruct(tile, BF16)] * parts,
            (me, comb, *halos[t], acc[t], noise_tiles), 1,
            scratch=[pltpu.VMEM((blocks * rows, LANES), F32), pltpu.VMEM((users, cells, 2 * blocks, LANES), BF16)],
        )
        got = [
            lax.ppermute(sent[d], "sc", [(i, (i + d) % parts) for i in range(parts)]) if d else sent[0] for d in range(parts)
        ]
        ins = (me, w1, twist, w2, *got) + (() if out is None else (out,))
        out = pl.pallas_call(
            functools.partial(time_kernel, t),
            grid=(1,),
            in_specs=[smem] + [whole(x.shape) for x in ins[1 : 4 + parts]] + [pl.BlockSpec(memory_space=pl.ANY)] * (t > 0),
            out_specs=pl.BlockSpec(full[:2] + (1,) + full[3:], lambda _, t=t: (0, 0, t, 0, 0)),
            out_shape=jax.ShapeDtypeStruct(full, BF16),
            input_output_aliases={4 + parts: 0} if t else {},
            name="time",
            compiler_params=pltpu.CompilerParams(vmem_limit_bytes=16 << 20),
            cost_estimate=pl.CostEstimate(flops=1_000_000_000, bytes_accessed=2_000_000, transcendentals=0),
        )(*ins)
    out = out.reshape(cells, share, times, length // LANES, 2, LANES).transpose(0, 1, 2, 4, 3, 5)
    return out.reshape(cells, share, times, 2, length)


def solution(mesh):
    in_specs = (
        P(("groups", "cell"), None, None, "sc"),
        P(("groups", "cell"), "sc", None, None),
        P(("groups", "cell")),
        P(("groups", "cell"), None, "sc", None),
        P(("groups", "cell"), None, None, "sc", None),
        P(("groups", "cell"), None),
        P(("groups", "cell"), None, None, None, "sc"),
    )
    out_specs = P(("groups", "cell"), "sc", None, None, None)
    return jax.shard_map(body, mesh=mesh, in_specs=in_specs, out_specs=out_specs, check_vma=False)
```

```python
import functools
import math

import jax
import jax.numpy as jnp
import numpy as np
from jax import lax
from jax.experimental import pallas as pl
from jax.experimental.pallas import tpu as pltpu
from jax.sharding import PartitionSpec as P

LANES = 128
SMEM = pltpu.MemorySpace.SMEM
BF16, F32 = jnp.bfloat16, jnp.float32
NT = (((1,), (1,)), ((), ()))


def gate_kernel(plan_ref, x_ref, *outs):
    cells, times, streams, _ = x_ref.shape
    for c in range(cells):
        on = plan_ref[c] != 0
        for t in range(times):
            x = x_ref[c, t]
            outs[t][c * streams : (c + 1) * streams] = jnp.where(on, x, jnp.zeros_like(x))


def place(near_ref, base_ref, total, cells, slots):
    table = []
    for c in range(cells):
        row = []
        for k in range(slots):
            at = near_ref[c, k] - base_ref[0] + cells
            at = jnp.where(at < 0, at + total, at)
            row.append(jnp.where(at >= total, at - total, at))
        table.append(row)
    return table


def combined_channel(masks, h, p):
    cells = p.shape[0]
    slots = len(masks[0])
    users = h.shape[0] // (slots * cells)
    half = p.shape[-1] // 2
    wide = p.astype(F32)
    lane = lax.broadcasted_iota(jnp.int32, wide.shape[1:], 1)
    p0 = [jnp.where(lane < half, wide[n], -wide[n]) for n in range(cells)]
    p1 = [pltpu.roll(wide[n], half, 1) for n in range(cells)]
    rows = [r for n in range(cells) for r in (p0[n], -p1[n])] + [r for n in range(cells) for r in (p1[n], p0[n])]
    rhs = jnp.concatenate(rows, axis=0).astype(BF16)
    prod = lax.dot_general(h, rhs, NT, preferred_element_type=F32)
    width = prod.shape[1] // 2
    out = []
    for z in range(2):
        for c in range(cells):
            acc = jnp.zeros((users, width), F32)
            for k in range(slots):
                start = (k * cells + c) * users
                part = prod[start : start + users, z * width : (z + 1) * width]
                acc = jnp.where(masks[c][k], part, acc)
            out.append(acc)
    return jnp.concatenate(out, axis=0).astype(BF16)


def source_masks(table, base, users, cells, width):
    source = lax.broadcasted_iota(jnp.int32, (users, width), 1) // (width // cells) + base
    return [[source == at for at in row] for row in table]


def pick_subbands(res, per):
    rows = res.shape[0] // per
    lane = lax.broadcasted_iota(jnp.int32, (rows, LANES), 1) // (LANES // per)
    out = res[:rows]
    for i in range(1, per):
        out = jnp.where(lane == i, res[i * rows : (i + 1) * rows], out)
    return out


def own_kernel(total, near_ref, base_ref, h_ref, own_ref, p_ref, *refs):
    times = len(refs) // 2
    s_refs, acc_refs = refs[:times], refs[times:]
    blocks, rows, _ = acc_refs[0].shape
    subbands, cells = p_ref.shape[1], p_ref.shape[0]
    per = subbands // blocks
    users = own_ref.shape[1] // cells
    table = place(near_ref, base_ref, total, cells, h_ref.shape[1] // (cells * users))
    table = [row + [cells + c] for c, row in enumerate(table)]
    masks = source_masks(table, cells, users, cells, s_refs[0].shape[0])
    for r in range(blocks):
        g = []
        for b in range(r * per, (r + 1) * per):
            h = jnp.concatenate([h_ref[b], own_ref[b]], axis=0)
            g.append(combined_channel(masks, h, p_ref[:, b]))
        g = jnp.concatenate(g, axis=0)
        for t in range(times):
            res = jnp.dot(g, s_refs[t][:, r * LANES : (r + 1) * LANES], preferred_element_type=F32)
            acc_refs[t][r] = pick_subbands(res, per)


def remote_kernel(total, users, near_ref, base_ref, h_ref, a_ref, b_ref, g_ref):
    subbands, cells = a_ref.shape[1], a_ref.shape[0]
    blocks = g_ref.shape[0]
    per = subbands // blocks
    width = g_ref.shape[2] // 2
    rows = 2 * cells * users
    table = place(near_ref, base_ref, total, cells, h_ref.shape[1] // (cells * users))
    for side, (ref, base) in enumerate(((a_ref, 0), (b_ref, 2 * cells))):
        masks = source_masks(table, base, users, cells, width)
        for b in range(subbands):
            r, i = divmod(b, per)
            g_ref[r, i * rows : (i + 1) * rows, side * width : (side + 1) * width] = combined_channel(
                masks, h_ref[b], ref[:, b]
            )


def grid_kernel(t, me_ref, g_ref, a_ref, b_ref, acc_ref, noise_ref, *refs):
    outs, y, turned, tiles = refs[:-3], refs[-3], refs[-2], refs[-1]
    blocks, rows, _ = acc_ref.shape
    per = g_ref.shape[1] // rows
    cells, users = noise_ref.shape[:2]
    for r in range(blocks):
        lanes = slice(r * LANES, (r + 1) * LANES)
        s = jnp.concatenate([a_ref[:, lanes], b_ref[:, lanes]], axis=0)
        res = jnp.dot(g_ref[r], s, preferred_element_type=F32)
        y[r * rows : (r + 1) * rows] = acc_ref[r] + pick_subbands(res, per)
    half = rows // 2
    step = 8
    for first in range(0, half, step):
        for part in range(2 * blocks // step):
            src = [divmod(part * step + i, 2) for i in range(step)]
            group = [y[r * rows + z * half + first : r * rows + z * half + first + step] for r, z in src]
            turned[part, first : first + step] = jnp.swapaxes(jnp.stack(group), 0, 1)
    for row in range(half):
        c, u = divmod(row, users)
        tile = jnp.concatenate([turned[part, row] for part in range(2 * blocks // step)], axis=0)
        tiles[u, c] = (tile + noise_ref[c, u, t].astype(F32)).astype(BF16)
    count = len(outs)
    for d in range(count):
        group = lax.rem(me_ref[0] + d, count)
        outs[d][...] = tiles[pl.ds(group * (users // count), users // count)]


def swap_groups(parts, width):
    parts = list(parts)
    lane = lax.broadcasted_iota(jnp.int32, parts[0].shape, 1)
    step = len(parts) // 2
    while step:
        low = (lane // (width * step)) % 2 == 0
        for i in range(len(parts)):
            if i & step == 0:
                x, y = parts[i], parts[i + step]
                parts[i] = jnp.where(low, x, pltpu.roll(y, width * step, 1))
                parts[i + step] = jnp.where(low, pltpu.roll(x, LANES - width * step, 1), y)
        step //= 2
    return parts


def time_kernel(t, me_ref, w1_ref, tw_ref, w2_ref, *refs):
    parts, (out_ref, held, sems) = refs[: w1_ref.shape[0]], refs[-3:]
    share, cells = parts[0].shape[:2]
    seqs = share * cells
    rows = tw_ref.shape[1]
    per = LANES // rows
    w1 = w1_ref[me_ref[0]]
    w2 = w2_ref[...]
    n2 = w2.shape[0] // 2
    tall = n2 // per
    batch = min(seqs, 2 * per)
    copies = []
    for first in range(0, seqs, batch):
        data = jnp.concatenate(
            [jnp.concatenate([p[q // cells, q % cells] for p in parts], axis=0) for q in range(first, first + batch)], axis=1
        )
        both = jnp.dot(w1, data, preferred_element_type=F32)
        both = both[: 2 * rows] + both[2 * rows :]
        turned = []
        for q in range(batch):
            re = both[:rows, q * LANES : (q + 1) * LANES]
            im = both[rows:, q * LANES : (q + 1) * LANES]
            turned.append(
                jnp.concatenate([re * tw_ref[0] - im * tw_ref[1], re * tw_ref[1] + im * tw_ref[0]], axis=1)
            )
        turned = jnp.concatenate(turned, axis=0)
        high = turned.astype(BF16)
        low = (turned - high.astype(F32)).astype(BF16)
        prod = lax.dot_general(w2, high, NT, preferred_element_type=F32)
        prod = prod[:n2] + prod[n2:] + lax.dot_general(w2[:n2], low, NT, preferred_element_type=F32)
        for quad in range(batch // per):
            lanes = slice(quad * LANES, (quad + 1) * LANES)
            pieces = swap_groups([prod[i * tall : (i + 1) * tall, lanes].astype(BF16) for i in range(per)], rows)
            for at, piece in enumerate(pieces):
                u, c = divmod(first + quad * per + at, cells)
                held[u, c] = piece
                if c == cells - 1:
                    copies.append(pltpu.make_async_copy(held.at[u], out_ref.at[:, u, t], sems.at[u]))
                    copies[-1].start()
    for copy in copies:
        copy.wait()


def rotation(angle):
    return np.block([[np.cos(angle), -np.sin(angle)], [np.sin(angle), np.cos(angle)]])


def split_rows(table):
    high = table.astype(jnp.bfloat16)
    low = (table - high.astype(np.float64)).astype(jnp.bfloat16)
    return np.concatenate([high, low], axis=0)


def tables(length, parts):
    rows = length // LANES
    local = rows // parts
    m = np.arange(rows)
    w1 = []
    for me in range(parts):
        order = np.concatenate([(me - d) % parts * local + np.arange(local) for d in range(parts)])
        angle = 2 * np.pi * (np.outer(m, order) % rows) / rows
        full = rotation(angle).reshape(2 * rows, 2, rows).transpose(0, 2, 1).reshape(2 * rows, 2 * rows)
        w1.append(split_rows(full))
    lane = np.arange(LANES)
    angle = 2 * np.pi * (np.outer(m, lane) % length) / length
    twist = (np.stack([np.cos(angle), np.sin(angle)]) / math.sqrt(length)).astype(np.float32)
    per = LANES // rows
    angle = 2 * np.pi * (np.outer(lane, lane) % LANES) / LANES
    w2 = rotation(angle).reshape(2, rows, per, 2 * LANES).transpose(2, 1, 0, 3).reshape(2 * LANES, 2 * LANES)
    return np.stack(w1), twist, split_rows(w2)


def body(symbols, precoders, plan, own_channel, cross_channel, neighbours, noise):
    cells, times, streams, width = symbols.shape
    subbands, users, slots, ants = precoders.shape[1], own_channel.shape[1], cross_channel.shape[2], precoders.shape[3]
    blocks = width // LANES
    per = subbands // blocks
    parts = lax.axis_size("sc")
    ring = lax.axis_size("cell")
    length = width * parts
    rows = 2 * cells * users
    up = [(i, (i + 1) % ring) for i in range(ring)]
    down = [(j, i) for i, j in up]

    def both_ways(x):
        return lax.ppermute(x, "cell", up), lax.ppermute(x, "cell", down)

    total = cells * ring
    tall = cells * streams
    vmem = pl.BlockSpec(memory_space=pltpu.MemorySpace.VMEM)
    smem = pl.BlockSpec(memory_space=SMEM)
    hbm = pl.BlockSpec(memory_space=pltpu.MemorySpace.HBM)

    def call(kernel, name, out_shape, ins, scalars, scratch=(), grant=16, flops=1_000_000_000, **more):
        return pl.pallas_call(
            kernel,
            in_specs=[smem] * scalars + [vmem] * (len(ins) - scalars),
            out_specs=jax.tree.map(lambda _: vmem, out_shape),
            out_shape=out_shape,
            scratch_shapes=scratch,
            name=name,
            compiler_params=pltpu.CompilerParams(vmem_limit_bytes=grant << 20),
            cost_estimate=pl.CostEstimate(flops=flops, bytes_accessed=4_000_000, transcendentals=0),
        )(*ins)

    p_before, p_after = both_ways(precoders)
    gated = call(gate_kernel, "gate", [jax.ShapeDtypeStruct((tall, width), BF16)] * times, (plan, symbols), 1)
    halos = [both_ways(g) for g in gated]

    base = (lax.axis_index("cell") * cells).astype(jnp.int32)[None]
    me = lax.axis_index("sc").astype(jnp.int32)[None]
    cross = cross_channel.transpose(3, 2, 0, 1, 4).reshape(subbands, slots * cells * users, ants)
    own = own_channel.transpose(2, 0, 1, 3).reshape(subbands, cells * users, ants)
    noise_tiles = noise.reshape(cells, users, times, 2, blocks, LANES).transpose(0, 1, 2, 4, 3, 5)
    noise_tiles = noise_tiles.reshape(cells, users, times, 2 * blocks, LANES)

    acc = call(
        functools.partial(own_kernel, total), "own_cells", [jax.ShapeDtypeStruct((blocks, rows, LANES), F32)] * times,
        (neighbours, base, cross, own, precoders, *gated), 2,
    )
    comb = call(
        functools.partial(remote_kernel, total, users), "other_cells",
        jax.ShapeDtypeStruct((blocks, per * rows, 2 * tall), BF16),
        (neighbours, base, cross, p_before, p_after), 2,
    )

    w1, twist, w2 = (jnp.asarray(x) for x in tables(length, parts))
    share = users // parts
    full = (cells, share, times, 2 * length // LANES, LANES)
    out = None
    for t in range(times):
        tile = (share, cells, 2 * blocks, LANES)
        sent = call(
            functools.partial(grid_kernel, t), "grid", [jax.ShapeDtypeStruct(tile, BF16)] * parts,
            (me, comb, *halos[t], acc[t], noise_tiles), 1,
            scratch=[
                pltpu.VMEM((blocks * rows, LANES), F32),
                pltpu.VMEM((2 * blocks // 8, rows // 2, 8, LANES), F32),
                pltpu.VMEM((users, cells, 2 * blocks, LANES), BF16),
            ],
        )
        got = [
            lax.ppermute(sent[d], "sc", [(i, (i + d) % parts) for i in range(parts)]) if d else sent[0] for d in range(parts)
        ]
        ins = (me, w1, twist, w2, *got) + (() if out is None else (out,))
        out = pl.pallas_call(
            functools.partial(time_kernel, t),
            in_specs=[smem] + [vmem] * (3 + parts) + [hbm] * (t > 0),
            out_specs=hbm,
            out_shape=jax.ShapeDtypeStruct(full, BF16),
            input_output_aliases={4 + parts: 0} if t else {},
            scratch_shapes=[
                pltpu.VMEM((share, cells, 2 * length // LANES, LANES), BF16),
                pltpu.SemaphoreType.DMA((share,)),
            ],
            name="time",
            compiler_params=pltpu.CompilerParams(vmem_limit_bytes=16 << 20),
            cost_estimate=pl.CostEstimate(flops=1_000_000_000, bytes_accessed=2_000_000, transcendentals=0),
        )(*ins)
    out = out.reshape(cells, share, times, length // LANES, 2, LANES).transpose(0, 1, 2, 4, 3, 5)
    return out.reshape(cells, share, times, 2, length)


def solution(mesh):
    in_specs = (
        P(("groups", "cell"), None, None, "sc"),
        P(("groups", "cell"), "sc", None, None),
        P(("groups", "cell")),
        P(("groups", "cell"), None, "sc", None),
        P(("groups", "cell"), None, None, "sc", None),
        P(("groups", "cell"), None),
        P(("groups", "cell"), None, None, None, "sc"),
    )
    out_specs = P(("groups", "cell"), "sc", None, None, None)
    return jax.shard_map(body, mesh=mesh, in_specs=in_specs, out_specs=out_specs, check_vma=False)
```

```python
import functools
import math

import jax
import jax.numpy as jnp
import numpy as np
from jax import lax
from jax.experimental import pallas as pl
from jax.experimental.pallas import tpu as pltpu
from jax.sharding import PartitionSpec as P

LANES = 128
SMEM = pltpu.MemorySpace.SMEM
BF16, F32 = jnp.bfloat16, jnp.float32
NT = (((1,), (1,)), ((), ()))


def partner(me, d, parts):
    return me ^ d if parts & (parts - 1) == 0 else (me + d) % parts


def gate_kernel(chunks, plan_ref, x_ref, *outs):
    cells, _, streams, _ = x_ref.shape
    for c in range(cells):
        on = plan_ref[c] != 0
        for out, (t, first, count) in zip(outs, chunks):
            x = x_ref[c, t, :, first * LANES : (first + count) * LANES]
            out[c * streams : (c + 1) * streams] = jnp.where(on, x, jnp.zeros_like(x))


def place(near_ref, base_ref, total, cells, slots):
    table = []
    for c in range(cells):
        row = []
        for k in range(slots):
            at = near_ref[c, k] - base_ref[0] + cells
            at = jnp.where(at < 0, at + total, at)
            row.append(jnp.where(at >= total, at - total, at))
        table.append(row)
    return table


def combined_channel(masks, h, p):
    cells = p.shape[0]
    slots = len(masks[0])
    users = h.shape[0] // (slots * cells)
    half = p.shape[-1] // 2
    wide = p.astype(F32)
    lane = lax.broadcasted_iota(jnp.int32, wide.shape[1:], 1)
    p0 = [jnp.where(lane < half, wide[n], -wide[n]) for n in range(cells)]
    p1 = [pltpu.roll(wide[n], half, 1) for n in range(cells)]
    rows = [r for n in range(cells) for r in (p0[n], -p1[n])] + [r for n in range(cells) for r in (p1[n], p0[n])]
    rhs = jnp.concatenate(rows, axis=0).astype(BF16)
    prod = lax.dot_general(h, rhs, NT, preferred_element_type=F32)
    width = prod.shape[1] // 2
    out = []
    for z in range(2):
        for c in range(cells):
            acc = jnp.zeros((users, width), F32)
            for k in range(slots):
                start = (k * cells + c) * users
                part = prod[start : start + users, z * width : (z + 1) * width]
                acc = jnp.where(masks[c][k], part, acc)
            out.append(acc)
    return jnp.concatenate(out, axis=0).astype(BF16)


def source_masks(table, base, users, cells, width):
    source = lax.broadcasted_iota(jnp.int32, (users, width), 1) // (width // cells) + base
    return [[source == at for at in row] for row in table]


def pick_subbands(res, per):
    rows = res.shape[0] // per
    lane = lax.broadcasted_iota(jnp.int32, (rows, LANES), 1) // (LANES // per)
    out = res[:rows]
    for i in range(1, per):
        out = jnp.where(lane == i, res[i * rows : (i + 1) * rows], out)
    return out


def own_kernel(total, chunks, near_ref, base_ref, h_ref, own_ref, p_ref, *refs):
    s_refs, acc_refs = refs[: len(chunks)], refs[len(chunks) :]
    rows = acc_refs[0].shape[1]
    blocks = max(first + count for _, first, count in chunks)
    subbands, cells = p_ref.shape[1], p_ref.shape[0]
    per = subbands // blocks
    users = own_ref.shape[1] // cells
    table = place(near_ref, base_ref, total, cells, h_ref.shape[1] // (cells * users))
    table = [row + [cells + c] for c, row in enumerate(table)]
    masks = source_masks(table, cells, users, cells, s_refs[0].shape[0])
    for r in range(blocks):
        g = []
        for b in range(r * per, (r + 1) * per):
            h = jnp.concatenate([h_ref[b], own_ref[b]], axis=0)
            g.append(combined_channel(masks, h, p_ref[:, b]))
        g = jnp.concatenate(g, axis=0)
        for s_ref, acc_ref, (_, first, count) in zip(s_refs, acc_refs, chunks):
            if first <= r < first + count:
                at = r - first
                res = jnp.dot(g, s_ref[:, at * LANES : (at + 1) * LANES], preferred_element_type=F32)
                acc_ref[at] = pick_subbands(res, per)


def remote_kernel(total, users, near_ref, base_ref, h_ref, a_ref, b_ref, g_ref):
    subbands, cells = a_ref.shape[1], a_ref.shape[0]
    blocks = g_ref.shape[0]
    per = subbands // blocks
    width = g_ref.shape[2] // 2
    rows = 2 * cells * users
    table = place(near_ref, base_ref, total, cells, h_ref.shape[1] // (cells * users))
    for side, (ref, base) in enumerate(((a_ref, 0), (b_ref, 2 * cells))):
        masks = source_masks(table, base, users, cells, width)
        for b in range(subbands):
            r, i = divmod(b, per)
            g_ref[r, i * rows : (i + 1) * rows, side * width : (side + 1) * width] = combined_channel(
                masks, h_ref[b], ref[:, b]
            )


def grid_kernel(chunk, me_ref, g_ref, a_ref, b_ref, acc_ref, noise_ref, *refs):
    outs, y, turned, tiles = refs[:-3], refs[-3], refs[-2], refs[-1]
    t, start, _ = chunk
    blocks, rows, _ = acc_ref.shape
    per = g_ref.shape[1] // rows
    cells, users = noise_ref.shape[:2]
    for r in range(blocks):
        lanes = slice(r * LANES, (r + 1) * LANES)
        s = jnp.concatenate([a_ref[:, lanes], b_ref[:, lanes]], axis=0)
        res = jnp.dot(g_ref[start + r], s, preferred_element_type=F32)
        y[r * rows : (r + 1) * rows] = acc_ref[r] + pick_subbands(res, per)
    half = rows // 2
    step = 8
    for first in range(0, half, step):
        for part in range(2 * blocks // step):
            src = [divmod(part * step + i, 2) for i in range(step)]
            group = [y[r * rows + z * half + first : r * rows + z * half + first + step] for r, z in src]
            turned[part, first : first + step] = jnp.swapaxes(jnp.stack(group), 0, 1)
    for row in range(half):
        c, u = divmod(row, users)
        tile = jnp.concatenate([turned[part, row] for part in range(2 * blocks // step)], axis=0)
        tiles[u, c] = (tile + noise_ref[c, u, t, 2 * start : 2 * (start + blocks)].astype(F32)).astype(BF16)
    count = len(outs)
    for d in range(count):
        group = partner(me_ref[0], d, count)
        outs[d][...] = tiles[pl.ds(group * (users // count), users // count)]


def swap_groups(parts, width):
    parts = list(parts)
    lane = lax.broadcasted_iota(jnp.int32, parts[0].shape, 1)
    step = len(parts) // 2
    while step:
        low = (lane // (width * step)) % 2 == 0
        for i in range(len(parts)):
            if i & step == 0:
                x, y = parts[i], parts[i + step]
                parts[i] = jnp.where(low, x, pltpu.roll(y, width * step, 1))
                parts[i + step] = jnp.where(low, pltpu.roll(x, LANES - width * step, 1), y)
        step //= 2
    return parts


def time_kernel(t, halves, w1_ref, tw_ref, w2_ref, *refs):
    out_ref, held, sems = refs[-3:]
    rows = tw_ref.shape[1]
    share, cells, tall, _ = refs[0].shape
    parts = refs[: 2 * rows // tall]
    seqs = share * cells
    per = LANES // rows
    w1 = w1_ref[...]
    w2 = w2_ref[...]
    n2 = w2.shape[0] // 2
    tall = n2 // per
    batch = min(seqs, 2 * per)
    held_as = BF16 if halves == 1 else F32
    copies = []
    for first in range(0, seqs, batch):
        data = [
            jnp.concatenate([p[q // cells, q % cells].astype(held_as) for p in parts], axis=0)
            for q in range(first, first + batch)
        ]
        data = jnp.concatenate(data, axis=1).astype(BF16)
        both = jnp.dot(w1, data, preferred_element_type=F32)
        both = both[: 2 * rows] + both[2 * rows :]
        turned = []
        for q in range(batch):
            re = both[:rows, q * LANES : (q + 1) * LANES]
            im = both[rows:, q * LANES : (q + 1) * LANES]
            turned.append(
                jnp.concatenate([re * tw_ref[0] - im * tw_ref[1], re * tw_ref[1] + im * tw_ref[0]], axis=1)
            )
        turned = jnp.concatenate(turned, axis=0)
        high = turned.astype(BF16)
        low = (turned - high.astype(F32)).astype(BF16)
        prod = lax.dot_general(w2, high, NT, preferred_element_type=F32)
        prod = prod[:n2] + prod[n2:] + lax.dot_general(w2[:n2], low, NT, preferred_element_type=F32)
        for quad in range(batch // per):
            lanes = slice(quad * LANES, (quad + 1) * LANES)
            pieces = swap_groups([prod[i * tall : (i + 1) * tall, lanes].astype(BF16) for i in range(per)], rows)
            for at, piece in enumerate(pieces):
                u, c = divmod(first + quad * per + at, cells)
                held[u, c] = piece
                if c == cells - 1:
                    copies.append(pltpu.make_async_copy(held.at[u], out_ref.at[:, u, t], sems.at[u]))
                    copies[-1].start()
    for copy in copies:
        copy.wait()


def rotation(angle):
    return np.block([[np.cos(angle), -np.sin(angle)], [np.sin(angle), np.cos(angle)]])


def split_rows(table):
    high = table.astype(jnp.bfloat16)
    low = (table - high.astype(np.float64)).astype(jnp.bfloat16)
    return np.concatenate([high, low], axis=0)


def tables(length, parts):
    rows = length // LANES
    local = rows // parts
    m = np.arange(rows)
    w1 = []
    for me in range(parts):
        source = [me ^ d if parts & (parts - 1) == 0 else (me - d) % parts for d in range(parts)]
        order = np.concatenate([src * local + np.arange(local) for src in source])
        angle = 2 * np.pi * (np.outer(m, order) % rows) / rows
        full = rotation(angle).reshape(2 * rows, 2, rows).transpose(0, 2, 1).reshape(2 * rows, 2 * rows)
        w1.append(split_rows(full))
    lane = np.arange(LANES)
    angle = 2 * np.pi * (np.outer(m, lane) % length) / length
    twist = (np.stack([np.cos(angle), np.sin(angle)]) / math.sqrt(length)).astype(np.float32)
    per = LANES // rows
    angle = 2 * np.pi * (np.outer(lane, lane) % LANES) / LANES
    w2 = rotation(angle).reshape(2, rows, per, 2 * LANES).transpose(2, 1, 0, 3).reshape(2 * LANES, 2 * LANES)
    return np.stack(w1), twist, split_rows(w2)


def body(symbols, precoders, plan, own_channel, cross_channel, neighbours, noise):
    cells, times, streams, width = symbols.shape
    subbands, users, slots, ants = precoders.shape[1], own_channel.shape[1], cross_channel.shape[2], precoders.shape[3]
    blocks = width // LANES
    per = subbands // blocks
    parts = lax.axis_size("sc")
    ring = lax.axis_size("cell")
    length = width * parts
    rows = 2 * cells * users
    up = [(i, (i + 1) % ring) for i in range(ring)]
    down = [(j, i) for i, j in up]

    def both_ways(x):
        return lax.ppermute(x, "cell", up), lax.ppermute(x, "cell", down)

    total = cells * ring
    tall = cells * streams
    vmem = pl.BlockSpec(memory_space=pltpu.MemorySpace.VMEM)
    smem = pl.BlockSpec(memory_space=SMEM)
    hbm = pl.BlockSpec(memory_space=pltpu.MemorySpace.HBM)

    def call(kernel, name, out_shape, ins, scalars, scratch=(), grant=16, flops=1_000_000_000, **more):
        return pl.pallas_call(
            kernel,
            in_specs=[smem] * scalars + [vmem] * (len(ins) - scalars),
            out_specs=jax.tree.map(lambda _: vmem, out_shape),
            out_shape=out_shape,
            scratch_shapes=scratch,
            name=name,
            compiler_params=pltpu.CompilerParams(vmem_limit_bytes=grant << 20),
            cost_estimate=pl.CostEstimate(flops=flops, bytes_accessed=4_000_000, transcendentals=0),
        )(*ins)

    p_before, p_after = both_ways(precoders)
    chunks = [(t, 0, blocks) for t in range(times - 1)]
    cut = blocks // 2
    chunks += [(times - 1, 0, cut), (times - 1, cut, blocks - cut)]
    gated = call(
        functools.partial(gate_kernel, chunks), "gate",
        [jax.ShapeDtypeStruct((tall, count * LANES), BF16) for _, _, count in chunks], (plan, symbols), 1,
    )
    halos = [both_ways(g) for g in gated]

    base = (lax.axis_index("cell") * cells).astype(jnp.int32)[None]
    me = lax.axis_index("sc").astype(jnp.int32)[None]
    cross = cross_channel.transpose(3, 2, 0, 1, 4).reshape(subbands, slots * cells * users, ants)
    own = own_channel.transpose(2, 0, 1, 3).reshape(subbands, cells * users, ants)
    noise_tiles = noise.reshape(cells, users, times, 2, blocks, LANES).transpose(0, 1, 2, 4, 3, 5)
    noise_tiles = noise_tiles.reshape(cells, users, times, 2 * blocks, LANES)

    acc = call(
        functools.partial(own_kernel, total, chunks), "own_cells",
        [jax.ShapeDtypeStruct((count, rows, LANES), F32) for _, _, count in chunks],
        (neighbours, base, cross, own, precoders, *gated), 2,
    )
    comb = call(
        functools.partial(remote_kernel, total, users), "other_cells",
        jax.ShapeDtypeStruct((blocks, per * rows, 2 * tall), BF16),
        (neighbours, base, cross, p_before, p_after), 2,
    )

    w1, twist, w2 = (jnp.asarray(x) for x in tables(length, parts))
    w1 = lax.dynamic_index_in_dim(w1, me[0], 0, False)
    share = users // parts
    full = (cells, share, times, 2 * length // LANES, LANES)
    out, got = None, []
    for at, (chunk, halo) in enumerate(zip(chunks, halos)):
        t, _, count = chunk
        tile = (share, cells, 2 * count, LANES)
        sent = call(
            functools.partial(grid_kernel, chunk), "grid", [jax.ShapeDtypeStruct(tile, BF16)] * parts,
            (me, comb, *halo, acc[at], noise_tiles), 1,
            scratch=[
                pltpu.VMEM((count * rows, LANES), F32),
                pltpu.VMEM((2 * count // 8, rows // 2, 8, LANES), F32),
                pltpu.VMEM((users, cells, 2 * count, LANES), BF16),
            ],
        )
        moved = {d: lax.ppermute(sent[d], "sc", [(i, int(partner(i, d, parts))) for i in range(parts)]) for d in range(parts - 1, 0, -1)}
        got.append([sent[0]] + [moved[d] for d in range(1, parts)])
        if at + 1 < len(chunks) and chunks[at + 1][0] == t:
            continue
        halves = len(got)
        arrived = [got[h][d] for d in range(parts) for h in range(halves)]
        got = []
        ins = (w1, twist, w2, *arrived) + (() if out is None else (out,))
        out = pl.pallas_call(
            functools.partial(time_kernel, t, halves),
            in_specs=[vmem] * (3 + len(arrived)) + [hbm] * (t > 0),
            out_specs=hbm,
            out_shape=jax.ShapeDtypeStruct(full, BF16),
            input_output_aliases={3 + len(arrived): 0} if t else {},
            scratch_shapes=[
                pltpu.VMEM((share, cells, 2 * length // LANES, LANES), BF16),
                pltpu.SemaphoreType.DMA((share,)),
            ],
            name="time",
            compiler_params=pltpu.CompilerParams(vmem_limit_bytes=16 << 20),
            cost_estimate=pl.CostEstimate(flops=1_000_000_000, bytes_accessed=2_000_000, transcendentals=0),
        )(*ins)
    out = out.reshape(cells, share, times, length // LANES, 2, LANES).transpose(0, 1, 2, 4, 3, 5)
    return out.reshape(cells, share, times, 2, length)


def solution(mesh):
    in_specs = (
        P(("groups", "cell"), None, None, "sc"),
        P(("groups", "cell"), "sc", None, None),
        P(("groups", "cell")),
        P(("groups", "cell"), None, "sc", None),
        P(("groups", "cell"), None, None, "sc", None),
        P(("groups", "cell"), None),
        P(("groups", "cell"), None, None, None, "sc"),
    )
    out_specs = P(("groups", "cell"), "sc", None, None, None)
    return jax.shard_map(body, mesh=mesh, in_specs=in_specs, out_specs=out_specs, check_vma=False)
```

```python
import functools
import math

import jax
import jax.numpy as jnp
import numpy as np
from jax import lax
from jax.experimental import pallas as pl
from jax.experimental.pallas import tpu as pltpu
from jax.sharding import PartitionSpec as P

LANES = 128
SMEM = pltpu.MemorySpace.SMEM
BF16, F32 = jnp.bfloat16, jnp.float32
NT = (((1,), (1,)), ((), ()))


def partner(me, d, parts):
    return (me + d) % parts


def gate_kernel(chunks, plan_ref, x_ref, *outs):
    cells, _, streams, _ = x_ref.shape
    for c in range(cells):
        on = plan_ref[c] != 0
        for out, (t, first, count) in zip(outs, chunks):
            x = x_ref[c, t, :, first * LANES : (first + count) * LANES]
            out[c * streams : (c + 1) * streams] = jnp.where(on, x, jnp.zeros_like(x))


def place(near_ref, base_ref, total, cells, slots):
    table = []
    for c in range(cells):
        row = []
        for k in range(slots):
            at = near_ref[c, k] - base_ref[0] + cells
            at = jnp.where(at < 0, at + total, at)
            row.append(jnp.where(at >= total, at - total, at))
        table.append(row)
    return table


def combined_channel(masks, h, p):
    cells = p.shape[0]
    slots = len(masks[0])
    users = h.shape[0] // (slots * cells)
    half = p.shape[-1] // 2
    wide = p.astype(F32)
    lane = lax.broadcasted_iota(jnp.int32, wide.shape[1:], 1)
    p0 = [jnp.where(lane < half, wide[n], -wide[n]) for n in range(cells)]
    p1 = [pltpu.roll(wide[n], half, 1) for n in range(cells)]
    rows = [r for n in range(cells) for r in (p0[n], -p1[n])] + [r for n in range(cells) for r in (p1[n], p0[n])]
    rhs = jnp.concatenate(rows, axis=0).astype(BF16)
    prod = lax.dot_general(h, rhs, NT, preferred_element_type=F32)
    width = prod.shape[1] // 2
    out = []
    for z in range(2):
        for c in range(cells):
            acc = jnp.zeros((users, width), F32)
            for k in range(slots):
                start = (k * cells + c) * users
                part = prod[start : start + users, z * width : (z + 1) * width]
                acc = jnp.where(masks[c][k], part, acc)
            out.append(acc)
    return jnp.concatenate(out, axis=0).astype(BF16)


def source_masks(table, base, users, cells, width):
    source = lax.broadcasted_iota(jnp.int32, (users, width), 1) // (width // cells) + base
    return [[source == at for at in row] for row in table]


def pick_subbands(res, per):
    rows = res.shape[0] // per
    lane = lax.broadcasted_iota(jnp.int32, (rows, LANES), 1) // (LANES // per)
    out = res[:rows]
    for i in range(1, per):
        out = jnp.where(lane == i, res[i * rows : (i + 1) * rows], out)
    return out


def own_kernel(total, chunks, near_ref, base_ref, h_ref, own_ref, p_ref, *refs):
    s_refs, acc_refs = refs[: len(chunks)], refs[len(chunks) :]
    rows = acc_refs[0].shape[1]
    blocks = max(first + count for _, first, count in chunks)
    subbands, cells = p_ref.shape[1], p_ref.shape[0]
    per = subbands // blocks
    users = own_ref.shape[1] // cells
    table = place(near_ref, base_ref, total, cells, h_ref.shape[1] // (cells * users))
    table = [row + [cells + c] for c, row in enumerate(table)]
    masks = source_masks(table, cells, users, cells, s_refs[0].shape[0])
    for r in range(blocks):
        g = []
        for b in range(r * per, (r + 1) * per):
            h = jnp.concatenate([h_ref[b], own_ref[b]], axis=0)
            g.append(combined_channel(masks, h, p_ref[:, b]))
        g = jnp.concatenate(g, axis=0)
        for s_ref, acc_ref, (_, first, count) in zip(s_refs, acc_refs, chunks):
            if first <= r < first + count:
                at = r - first
                res = jnp.dot(g, s_ref[:, at * LANES : (at + 1) * LANES], preferred_element_type=F32)
                acc_ref[at] = pick_subbands(res, per)


def remote_kernel(total, users, near_ref, base_ref, h_ref, a_ref, b_ref, g_ref):
    subbands, cells = a_ref.shape[1], a_ref.shape[0]
    blocks = g_ref.shape[0]
    per = subbands // blocks
    width = g_ref.shape[2] // 2
    rows = 2 * cells * users
    table = place(near_ref, base_ref, total, cells, h_ref.shape[1] // (cells * users))
    for side, (ref, base) in enumerate(((a_ref, 0), (b_ref, 2 * cells))):
        masks = source_masks(table, base, users, cells, width)
        for b in range(subbands):
            r, i = divmod(b, per)
            g_ref[r, i * rows : (i + 1) * rows, side * width : (side + 1) * width] = combined_channel(
                masks, h_ref[b], ref[:, b]
            )


def grid_kernel(chunk, me_ref, g_ref, a_ref, b_ref, acc_ref, noise_ref, *refs):
    outs, y, turned, tiles = refs[:-3], refs[-3], refs[-2], refs[-1]
    t, start, _ = chunk
    blocks, rows, _ = acc_ref.shape
    per = g_ref.shape[1] // rows
    cells, users = noise_ref.shape[:2]
    for r in range(blocks):
        lanes = slice(r * LANES, (r + 1) * LANES)
        s = jnp.concatenate([a_ref[:, lanes], b_ref[:, lanes]], axis=0)
        res = jnp.dot(g_ref[start + r], s, preferred_element_type=F32)
        y[r * rows : (r + 1) * rows] = acc_ref[r] + pick_subbands(res, per)
    half = rows // 2
    step = 8
    for first in range(0, half, step):
        for part in range(2 * blocks // step):
            src = [divmod(part * step + i, 2) for i in range(step)]
            group = [y[r * rows + z * half + first : r * rows + z * half + first + step] for r, z in src]
            turned[part, first : first + step] = jnp.swapaxes(jnp.stack(group), 0, 1)
    for row in range(half):
        c, u = divmod(row, users)
        tile = jnp.concatenate([turned[part, row] for part in range(2 * blocks // step)], axis=0)
        tiles[u, c] = (tile + noise_ref[c, u, t, 2 * start : 2 * (start + blocks)].astype(F32)).astype(BF16)
    count = len(outs)
    for d in range(count):
        group = partner(me_ref[0], d, count)
        outs[d][...] = tiles[pl.ds(group * (users // count), users // count)]


def swap_groups(parts, width):
    parts = list(parts)
    lane = lax.broadcasted_iota(jnp.int32, parts[0].shape, 1)
    step = len(parts) // 2
    while step:
        low = (lane // (width * step)) % 2 == 0
        for i in range(len(parts)):
            if i & step == 0:
                x, y = parts[i], parts[i + step]
                parts[i] = jnp.where(low, x, pltpu.roll(y, width * step, 1))
                parts[i + step] = jnp.where(low, pltpu.roll(x, LANES - width * step, 1), y)
        step //= 2
    return parts


def time_kernel(t, halves, w1_ref, tw_ref, w2_ref, *refs):
    out_ref, held, sems = refs[-3:]
    rows = tw_ref.shape[1]
    share, cells, tall, _ = refs[0].shape
    parts = refs[: 2 * rows // tall]
    seqs = share * cells
    per = LANES // rows
    w1 = w1_ref[...]
    w2 = w2_ref[...]
    n2 = w2.shape[0] // 2
    tall = n2 // per
    batch = min(seqs, 2 * per)
    held_as = BF16 if halves == 1 else F32
    copies = []
    for first in range(0, seqs, batch):
        data = [
            jnp.concatenate([p[q // cells, q % cells].astype(held_as) for p in parts], axis=0)
            for q in range(first, first + batch)
        ]
        data = jnp.concatenate(data, axis=1).astype(BF16)
        both = jnp.dot(w1, data, preferred_element_type=F32)
        both = both[: 2 * rows] + both[2 * rows :]
        turned = []
        for q in range(batch):
            re = both[:rows, q * LANES : (q + 1) * LANES]
            im = both[rows:, q * LANES : (q + 1) * LANES]
            turned.append(
                jnp.concatenate([re * tw_ref[0] - im * tw_ref[1], re * tw_ref[1] + im * tw_ref[0]], axis=1)
            )
        turned = jnp.concatenate(turned, axis=0)
        high = turned.astype(BF16)
        low = (turned - high.astype(F32)).astype(BF16)
        prod = lax.dot_general(w2, high, NT, preferred_element_type=F32)
        prod = prod[:n2] + prod[n2:] + lax.dot_general(w2[:n2], low, NT, preferred_element_type=F32)
        for quad in range(batch // per):
            lanes = slice(quad * LANES, (quad + 1) * LANES)
            pieces = swap_groups([prod[i * tall : (i + 1) * tall, lanes].astype(BF16) for i in range(per)], rows)
            for at, piece in enumerate(pieces):
                u, c = divmod(first + quad * per + at, cells)
                held[u, c] = piece
                if c == cells - 1:
                    copies.append(pltpu.make_async_copy(held.at[u], out_ref.at[:, u, t], sems.at[u]))
                    copies[-1].start()
    for copy in copies:
        copy.wait()


def rotation(angle):
    return np.block([[np.cos(angle), -np.sin(angle)], [np.sin(angle), np.cos(angle)]])


def split_rows(table):
    high = table.astype(jnp.bfloat16)
    low = (table - high.astype(np.float64)).astype(jnp.bfloat16)
    return np.concatenate([high, low], axis=0)


def tables(length, parts):
    rows = length // LANES
    local = rows // parts
    m = np.arange(rows)
    w1 = []
    for me in range(parts):
        source = [(me - d) % parts for d in range(parts)]
        order = np.concatenate([src * local + np.arange(local) for src in source])
        angle = 2 * np.pi * (np.outer(m, order) % rows) / rows
        full = rotation(angle).reshape(2 * rows, 2, rows).transpose(0, 2, 1).reshape(2 * rows, 2 * rows)
        w1.append(split_rows(full))
    lane = np.arange(LANES)
    angle = 2 * np.pi * (np.outer(m, lane) % length) / length
    twist = (np.stack([np.cos(angle), np.sin(angle)]) / math.sqrt(length)).astype(np.float32)
    per = LANES // rows
    angle = 2 * np.pi * (np.outer(lane, lane) % LANES) / LANES
    w2 = rotation(angle).reshape(2, rows, per, 2 * LANES).transpose(2, 1, 0, 3).reshape(2 * LANES, 2 * LANES)
    return np.stack(w1), twist, split_rows(w2)


def body(symbols, precoders, plan, own_channel, cross_channel, neighbours, noise):
    cells, times, streams, width = symbols.shape
    subbands, users, slots, ants = precoders.shape[1], own_channel.shape[1], cross_channel.shape[2], precoders.shape[3]
    blocks = width // LANES
    per = subbands // blocks
    parts = lax.axis_size("sc")
    ring = lax.axis_size("cell")
    length = width * parts
    rows = 2 * cells * users
    up = [(i, (i + 1) % ring) for i in range(ring)]
    down = [(j, i) for i, j in up]

    def both_ways(x):
        return lax.ppermute(x, "cell", up), lax.ppermute(x, "cell", down)

    total = cells * ring
    tall = cells * streams
    vmem = pl.BlockSpec(memory_space=pltpu.MemorySpace.VMEM)
    smem = pl.BlockSpec(memory_space=SMEM)
    hbm = pl.BlockSpec(memory_space=pltpu.MemorySpace.HBM)

    def call(kernel, name, out_shape, ins, scalars, scratch=(), grant=16, flops=1_000_000_000, **more):
        return pl.pallas_call(
            kernel,
            in_specs=[smem] * scalars + [vmem] * (len(ins) - scalars),
            out_specs=jax.tree.map(lambda _: vmem, out_shape),
            out_shape=out_shape,
            scratch_shapes=scratch,
            name=name,
            compiler_params=pltpu.CompilerParams(vmem_limit_bytes=grant << 20),
            cost_estimate=pl.CostEstimate(flops=flops, bytes_accessed=4_000_000, transcendentals=0),
        )(*ins)

    p_before, p_after = both_ways(precoders)
    chunks = [(t, 0, blocks) for t in range(times - 1)]
    cut = blocks // 2
    chunks += [(times - 1, 0, cut), (times - 1, cut, blocks - cut)]
    gated = call(
        functools.partial(gate_kernel, chunks), "gate",
        [jax.ShapeDtypeStruct((tall, count * LANES), BF16) for _, _, count in chunks], (plan, symbols), 1,
    )
    halos = [both_ways(g) for g in gated]

    base = (lax.axis_index("cell") * cells).astype(jnp.int32)[None]
    me = lax.axis_index("sc").astype(jnp.int32)[None]
    cross = cross_channel.transpose(3, 2, 0, 1, 4).reshape(subbands, slots * cells * users, ants)
    own = own_channel.transpose(2, 0, 1, 3).reshape(subbands, cells * users, ants)
    noise_tiles = noise.reshape(cells, users, times, 2, blocks, LANES).transpose(0, 1, 2, 4, 3, 5)
    noise_tiles = noise_tiles.reshape(cells, users, times, 2 * blocks, LANES)

    acc = call(
        functools.partial(own_kernel, total, chunks), "own_cells",
        [jax.ShapeDtypeStruct((count, rows, LANES), F32) for _, _, count in chunks],
        (neighbours, base, cross, own, precoders, *gated), 2,
    )
    comb = call(
        functools.partial(remote_kernel, total, users), "other_cells",
        jax.ShapeDtypeStruct((blocks, per * rows, 2 * tall), BF16),
        (neighbours, base, cross, p_before, p_after), 2,
    )

    w1, twist, w2 = (jnp.asarray(x) for x in tables(length, parts))
    w1 = lax.dynamic_index_in_dim(w1, me[0], 0, False)
    share = users // parts
    full = (cells, share, times, 2 * length // LANES, LANES)
    out, got = None, []
    for at, (chunk, halo) in enumerate(zip(chunks, halos)):
        t, _, count = chunk
        tile = (share, cells, 2 * count, LANES)
        sent = call(
            functools.partial(grid_kernel, chunk), "grid", [jax.ShapeDtypeStruct(tile, BF16)] * parts,
            (me, comb, *halo, acc[at], noise_tiles), 1,
            scratch=[
                pltpu.VMEM((count * rows, LANES), F32),
                pltpu.VMEM((2 * count // 8, rows // 2, 8, LANES), F32),
                pltpu.VMEM((users, cells, 2 * count, LANES), BF16),
            ],
        )
        moved = {d: lax.ppermute(sent[d], "sc", [(i, (i ^ d) if ([0, 0, 0])[at] else (i + d) % parts) for i in range(parts)]) for d in ([(3,2,1),(3,2,1),(2,1,3)])[at]}
        got.append([sent[0]] + [moved[d] for d in range(1, parts)])
        if at + 1 < len(chunks) and chunks[at + 1][0] == t:
            continue
        halves = len(got)
        arrived = [got[h][d] for d in range(parts) for h in range(halves)]
        got = []
        ins = (w1, twist, w2, *arrived) + (() if out is None else (out,))
        out = pl.pallas_call(
            functools.partial(time_kernel, t, halves),
            in_specs=[vmem] * (3 + len(arrived)) + [hbm] * (t > 0),
            out_specs=hbm,
            out_shape=jax.ShapeDtypeStruct(full, BF16),
            input_output_aliases={3 + len(arrived): 0} if t else {},
            scratch_shapes=[
                pltpu.VMEM((share, cells, 2 * length // LANES, LANES), BF16),
                pltpu.SemaphoreType.DMA((share,)),
            ],
            name="time",
            compiler_params=pltpu.CompilerParams(vmem_limit_bytes=16 << 20),
            cost_estimate=pl.CostEstimate(flops=1_000_000_000, bytes_accessed=2_000_000, transcendentals=0),
        )(*ins)
    out = out.reshape(cells, share, times, length // LANES, 2, LANES).transpose(0, 1, 2, 4, 3, 5)
    return out.reshape(cells, share, times, 2, length)


def solution(mesh):
    in_specs = (
        P(("groups", "cell"), None, None, "sc"),
        P(("groups", "cell"), "sc", None, None),
        P(("groups", "cell")),
        P(("groups", "cell"), None, "sc", None),
        P(("groups", "cell"), None, None, "sc", None),
        P(("groups", "cell"), None),
        P(("groups", "cell"), None, None, None, "sc"),
    )
    out_specs = P(("groups", "cell"), "sc", None, None, None)
    return jax.shard_map(body, mesh=mesh, in_specs=in_specs, out_specs=out_specs, check_vma=False)
```

```python
import functools
import math

import jax
import jax.numpy as jnp
import numpy as np
from jax import lax
from jax.experimental import pallas as pl
from jax.experimental.pallas import tpu as pltpu
from jax.sharding import PartitionSpec as P


LANES = 128
SMEM = pltpu.MemorySpace.SMEM
BF16, F32 = jnp.bfloat16, jnp.float32
NT = (((1,), (1,)), ((), ()))


def partner(me, d, parts):
    return (me + d) % parts


def gate_kernel(chunks, plan_ref, x_ref, *outs):
    cells, _, streams, _ = x_ref.shape
    for c in range(cells):
        on = plan_ref[c] != 0
        for out, (t, first, count) in zip(outs, chunks):
            x = x_ref[c, t, :, first * LANES : (first + count) * LANES]
            out[c * streams : (c + 1) * streams] = jnp.where(on, x, jnp.zeros_like(x))


def place(near_ref, base_ref, total, cells, slots):
    table = []
    for c in range(cells):
        row = []
        for k in range(slots):
            at = near_ref[c, k] - base_ref[0] + cells
            at = jnp.where(at < 0, at + total, at)
            row.append(jnp.where(at >= total, at - total, at))
        table.append(row)
    return table


def combined_channel(masks, h, p):
    cells = p.shape[0]
    slots = len(masks[0])
    users = h.shape[0] // (slots * cells)
    half = p.shape[-1] // 2
    wide = p.astype(F32)
    lane = lax.broadcasted_iota(jnp.int32, wide.shape[1:], 1)
    p0 = [jnp.where(lane < half, wide[n], -wide[n]) for n in range(cells)]
    p1 = [pltpu.roll(wide[n], half, 1) for n in range(cells)]
    rows = [r for n in range(cells) for r in (p0[n], -p1[n])] + [r for n in range(cells) for r in (p1[n], p0[n])]
    rhs = jnp.concatenate(rows, axis=0).astype(BF16)
    prod = lax.dot_general(h, rhs, NT, preferred_element_type=F32)
    width = prod.shape[1] // 2
    out = []
    for z in range(2):
        for c in range(cells):
            acc = jnp.zeros((users, width), F32)
            for k in range(slots):
                start = (k * cells + c) * users
                part = prod[start : start + users, z * width : (z + 1) * width]
                acc = jnp.where(masks[c][k], part, acc)
            out.append(acc)
    return jnp.concatenate(out, axis=0).astype(BF16)


def source_masks(table, base, users, cells, width):
    source = lax.broadcasted_iota(jnp.int32, (users, width), 1) // (width // cells) + base
    return [[source == at for at in row] for row in table]


def pick_subbands(res, per):
    rows = res.shape[0] // per
    lane = lax.broadcasted_iota(jnp.int32, (rows, LANES), 1) // (LANES // per)
    out = res[:rows]
    for i in range(1, per):
        out = jnp.where(lane == i, res[i * rows : (i + 1) * rows], out)
    return out


def own_kernel(total, chunks, near_ref, base_ref, h_ref, own_ref, p_ref, *refs):
    s_refs, acc_refs = refs[: len(chunks)], refs[len(chunks) :]
    blocks = max(first + count for _, first, count in chunks)
    subbands, cells = p_ref.shape[1], p_ref.shape[0]
    per = subbands // blocks
    users = own_ref.shape[1] // cells
    table = place(near_ref, base_ref, total, cells, h_ref.shape[1] // (cells * users))
    table = [row + [cells + c] for c, row in enumerate(table)]
    masks = source_masks(table, cells, users, cells, s_refs[0].shape[0])
    for r in range(blocks):
        g = []
        for b in range(r * per, (r + 1) * per):
            h = jnp.concatenate([h_ref[b], own_ref[b]], axis=0)
            g.append(combined_channel(masks, h, p_ref[:, b]))
        g = jnp.concatenate(g, axis=0)
        for s_ref, acc_ref, (_, first, count) in zip(s_refs, acc_refs, chunks):
            if first <= r < first + count:
                at = r - first
                res = jnp.dot(g, s_ref[:, at * LANES : (at + 1) * LANES], preferred_element_type=F32)
                acc_ref[at] = pick_subbands(res, per)


def remote_kernel(total, users, near_ref, base_ref, h_ref, a_ref, b_ref, g_ref):
    subbands, cells = a_ref.shape[1], a_ref.shape[0]
    blocks = g_ref.shape[0]
    per = subbands // blocks
    width = g_ref.shape[2] // 2
    rows = 2 * cells * users
    table = place(near_ref, base_ref, total, cells, h_ref.shape[1] // (cells * users))
    for side, (ref, base) in enumerate(((a_ref, 0), (b_ref, 2 * cells))):
        masks = source_masks(table, base, users, cells, width)
        for b in range(subbands):
            r, i = divmod(b, per)
            g_ref[r, i * rows : (i + 1) * rows, side * width : (side + 1) * width] = combined_channel(
                masks, h_ref[b], ref[:, b]
            )


def grid_kernel(chunk, me_ref, g_ref, a_ref, b_ref, acc_ref, noise_ref, *refs):
    outs, y, turned, tiles = refs[:-3], refs[-3], refs[-2], refs[-1]
    t, start, _ = chunk
    blocks, rows, _ = acc_ref.shape
    per = g_ref.shape[1] // rows
    _, users = noise_ref.shape[:2]
    for r in range(blocks):
        lanes = slice(r * LANES, (r + 1) * LANES)
        s = jnp.concatenate([a_ref[:, lanes], b_ref[:, lanes]], axis=0)
        res = jnp.dot(g_ref[start + r], s, preferred_element_type=F32)
        y[r * rows : (r + 1) * rows] = acc_ref[r] + pick_subbands(res, per)
    half = rows // 2
    step = 8
    for first in range(0, half, step):
        for part in range(2 * blocks // step):
            src = [divmod(part * step + i, 2) for i in range(step)]
            group = [y[r * rows + z * half + first : r * rows + z * half + first + step] for r, z in src]
            turned[part, first : first + step] = jnp.swapaxes(jnp.stack(group), 0, 1)
    for row in range(half):
        c, u = divmod(row, users)
        tile = jnp.concatenate([turned[part, row] for part in range(2 * blocks // step)], axis=0)
        tiles[u, c] = (tile + noise_ref[c, u, t, 2 * start : 2 * (start + blocks)].astype(F32)).astype(BF16)
    count = len(outs)
    for d in range(count):
        group = partner(me_ref[0], d, count)
        outs[d][...] = tiles[pl.ds(group * (users // count), users // count)]


def swap_groups(parts, width):
    parts = list(parts)
    lane = lax.broadcasted_iota(jnp.int32, parts[0].shape, 1)
    step = len(parts) // 2
    while step:
        low = (lane // (width * step)) % 2 == 0
        for i in range(len(parts)):
            if i & step == 0:
                x, y = parts[i], parts[i + step]
                parts[i] = jnp.where(low, x, pltpu.roll(y, width * step, 1))
                parts[i + step] = jnp.where(low, pltpu.roll(x, LANES - width * step, 1), y)
        step //= 2
    return parts


def time_kernel(t, halves, w1_ref, tw_ref, w2_ref, *refs):
    out_ref, held, sems = refs[-3:]
    rows = tw_ref.shape[1]
    share, cells, tall, _ = refs[0].shape
    parts = refs[: 2 * rows // tall]
    seqs = share * cells
    per = LANES // rows
    w1 = w1_ref[...]
    w2 = w2_ref[...]
    n2 = w2.shape[0] // 2
    tall = n2 // per
    batch = min(seqs, 2 * per)
    held_as = BF16 if halves == 1 else F32
    copies = []
    for first in range(0, seqs, batch):
        data = [
            jnp.concatenate([p[q // cells, q % cells].astype(held_as) for p in parts], axis=0)
            for q in range(first, first + batch)
        ]
        data = jnp.concatenate(data, axis=1).astype(BF16)
        both = jnp.dot(w1, data, preferred_element_type=F32)
        both = both[: 2 * rows] + both[2 * rows :]
        turned = []
        for q in range(batch):
            re = both[:rows, q * LANES : (q + 1) * LANES]
            im = both[rows:, q * LANES : (q + 1) * LANES]
            turned.append(
                jnp.concatenate([re * tw_ref[0] - im * tw_ref[1], re * tw_ref[1] + im * tw_ref[0]], axis=1)
            )
        turned = jnp.concatenate(turned, axis=0)
        high = turned.astype(BF16)
        low = (turned - high.astype(F32)).astype(BF16)
        prod = lax.dot_general(w2, high, NT, preferred_element_type=F32)
        prod = prod[:n2] + prod[n2:] + lax.dot_general(w2[:n2], low, NT, preferred_element_type=F32)
        for quad in range(batch // per):
            lanes = slice(quad * LANES, (quad + 1) * LANES)
            pieces = swap_groups([prod[i * tall : (i + 1) * tall, lanes].astype(BF16) for i in range(per)], rows)
            for at, piece in enumerate(pieces):
                u, c = divmod(first + quad * per + at, cells)
                held[u, c] = piece
                if c == cells - 1:
                    copies.append(pltpu.make_async_copy(held.at[u], out_ref.at[:, u, t], sems.at[u]))
                    copies[-1].start()
    for copy in copies:
        copy.wait()


def rotation(angle):
    return np.block([[np.cos(angle), -np.sin(angle)], [np.sin(angle), np.cos(angle)]])


def split_rows(table):
    high = table.astype(jnp.bfloat16)
    low = (table - high.astype(np.float64)).astype(jnp.bfloat16)
    return np.concatenate([high, low], axis=0)


def tables(length, parts):
    rows = length // LANES
    local = rows // parts
    m = np.arange(rows)
    w1 = []
    for me in range(parts):
        source = [(me - d) % parts for d in range(parts)]
        order = np.concatenate([src * local + np.arange(local) for src in source])
        angle = 2 * np.pi * (np.outer(m, order) % rows) / rows
        full = rotation(angle).reshape(2 * rows, 2, rows).transpose(0, 2, 1).reshape(2 * rows, 2 * rows)
        w1.append(split_rows(full))
    lane = np.arange(LANES)
    angle = 2 * np.pi * (np.outer(m, lane) % length) / length
    twist = (np.stack([np.cos(angle), np.sin(angle)]) / math.sqrt(length)).astype(np.float32)
    per = LANES // rows
    angle = 2 * np.pi * (np.outer(lane, lane) % LANES) / LANES
    w2 = rotation(angle).reshape(2, rows, per, 2 * LANES).transpose(2, 1, 0, 3).reshape(2 * LANES, 2 * LANES)
    return np.stack(w1), twist, split_rows(w2)


def body(symbols, precoders, plan, own_channel, cross_channel, neighbours, noise):
    cells, times, streams, width = symbols.shape
    subbands, users, slots, ants = precoders.shape[1], own_channel.shape[1], cross_channel.shape[2], precoders.shape[3]
    blocks = width // LANES
    per = subbands // blocks
    parts = lax.axis_size("sc")
    ring = lax.axis_size("cell")
    length = width * parts
    rows = 2 * cells * users
    up = [(i, (i + 1) % ring) for i in range(ring)]
    down = [(j, i) for i, j in up]

    def both_ways(x):
        moved = []
        for pairs in (up, down):
            moved.append(lax.ppermute(x, "cell", pairs))
        return moved

    total = cells * ring
    tall = cells * streams
    vmem = pl.BlockSpec(memory_space=pltpu.MemorySpace.VMEM)
    smem = pl.BlockSpec(memory_space=SMEM)
    hbm = pl.BlockSpec(memory_space=pltpu.MemorySpace.HBM)

    def call(kernel, out_shape, ins, scalars, scratch=(), grant=16, flops=1_000_000_000, **more):
        return pl.pallas_call(
            kernel,
            in_specs=[smem] * scalars + [vmem] * (len(ins) - scalars),
            out_specs=jax.tree.map(lambda _: vmem, out_shape),
            out_shape=out_shape,
            scratch_shapes=scratch,
            compiler_params=pltpu.CompilerParams(vmem_limit_bytes=grant << 20),
            cost_estimate=pl.CostEstimate(flops=flops, bytes_accessed=4_000_000, transcendentals=0),
        )(*ins)

    p_before, p_after = both_ways(precoders)
    chunks = [(t, 0, blocks) for t in range(times - 1)]
    cut = blocks // 2
    chunks += [(times - 1, 0, cut), (times - 1, cut, blocks - cut)]
    gated = call(
        functools.partial(gate_kernel, chunks),
        [jax.ShapeDtypeStruct((tall, count * LANES), BF16) for _, _, count in chunks], (plan, symbols), 1,
    )
    halos = [both_ways(g) for g in gated]

    base = (lax.axis_index("cell") * cells).astype(jnp.int32)[None]
    me = lax.axis_index("sc").astype(jnp.int32)[None]
    cross = cross_channel.transpose(3, 2, 0, 1, 4).reshape(subbands, slots * cells * users, ants)
    own = own_channel.transpose(2, 0, 1, 3).reshape(subbands, cells * users, ants)
    noise_tiles = noise.reshape(cells, users, times, 2, blocks, LANES).transpose(0, 1, 2, 4, 3, 5)
    noise_tiles = noise_tiles.reshape(cells, users, times, 2 * blocks, LANES)

    acc = call(
        functools.partial(own_kernel, total, chunks),
        [jax.ShapeDtypeStruct((count, rows, LANES), F32) for _, _, count in chunks],
        (neighbours, base, cross, own, precoders, *gated), 2,
    )
    comb = call(
        functools.partial(remote_kernel, total, users),
        jax.ShapeDtypeStruct((blocks, per * rows, 2 * tall), BF16),
        (neighbours, base, cross, p_before, p_after), 2,
    )

    w1, twist, w2 = (jnp.asarray(x) for x in tables(length, parts))
    w1 = lax.dynamic_index_in_dim(w1, me[0], 0, False)
    share = users // parts
    full = (cells, share, times, 2 * length // LANES, LANES)
    out, got = None, []
    for at, (chunk, halo) in enumerate(zip(chunks, halos)):
        t, _, count = chunk
        tile = (share, cells, 2 * count, LANES)
        sent = call(
            functools.partial(grid_kernel, chunk), [jax.ShapeDtypeStruct(tile, BF16)] * parts,
            (me, comb, *halo, acc[at], noise_tiles), 1,
            scratch=[
                pltpu.VMEM((count * rows, LANES), F32),
                pltpu.VMEM((2 * count // 8, rows // 2, 8, LANES), F32),
                pltpu.VMEM((users, cells, 2 * count, LANES), BF16),
            ],
        )
        moved = {d: lax.ppermute(sent[d], "sc", [(i, (i ^ d) if ([0, 0, 0])[at] else (i + d) % parts) for i in range(parts)]) for d in ([(3,2,1),(3,2,1),(2,1,3)])[at]}
        got.append([sent[0]] + [moved[d] for d in range(1, parts)])
        if at + 1 < len(chunks) and chunks[at + 1][0] == t:
            continue
        halves = len(got)
        arrived = [got[h][d] for d in range(parts) for h in range(halves)]
        got = []
        ins = (w1, twist, w2, *arrived) + (() if out is None else (out,))
        out = pl.pallas_call(
            functools.partial(time_kernel, t, halves),
            in_specs=[vmem] * (3 + len(arrived)) + [hbm] * (t > 0),
            out_specs=hbm,
            out_shape=jax.ShapeDtypeStruct(full, BF16),
            input_output_aliases={3 + len(arrived): 0} if t else {},
            scratch_shapes=[
                pltpu.VMEM((share, cells, 2 * length // LANES, LANES), BF16),
                pltpu.SemaphoreType.DMA((share,)),
            ],
            name="time",
            compiler_params=pltpu.CompilerParams(vmem_limit_bytes=16 << 20),
            cost_estimate=pl.CostEstimate(flops=1_000_000_000, bytes_accessed=2_000_000, transcendentals=0),
        )(*ins)
    out = out.reshape(cells, share, times, length // LANES, 2, LANES).transpose(0, 1, 2, 4, 3, 5)
    return out.reshape(cells, share, times, 2, length)


def solution(mesh):
    in_specs = (
        P(("groups", "cell"), None, None, "sc"),
        P(("groups", "cell"), "sc", None, None),
        P(("groups", "cell")),
        P(("groups", "cell"), None, "sc", None),
        P(("groups", "cell"), None, None, "sc", None),
        P(("groups", "cell"), None),
        P(("groups", "cell"), None, None, None, "sc"),
    )
    out_specs = P(("groups", "cell"), "sc", None, None, None)
    return jax.shard_map(body, mesh=mesh, in_specs=in_specs, out_specs=out_specs, check_vma=False)
```

```python
import functools
import math

import jax
import jax.numpy as jnp
import numpy as np
from jax import lax
from jax.experimental import pallas as pl
from jax.experimental.pallas import tpu as pltpu
from jax.sharding import PartitionSpec as P


LANES = 128
SMEM = pltpu.MemorySpace.SMEM
BF16, F32 = jnp.bfloat16, jnp.float32
NT = (((1,), (1,)), ((), ()))


def partner(me, d, parts):
    return (me + d) % parts


def gate_kernel(chunks, plan_ref, x_ref, *outs):
    cells, _, streams, _ = x_ref.shape
    for c in range(cells):
        on = plan_ref[c] != 0
        for out, (t, first, count) in zip(outs, chunks):
            x = x_ref[c, t, :, first * LANES : (first + count) * LANES]
            out[c * streams : (c + 1) * streams] = jnp.where(on, x, jnp.zeros_like(x))


def place(near_ref, base_ref, total, cells, slots):
    table = []
    for c in range(cells):
        row = []
        for k in range(slots):
            at = near_ref[c, k] - base_ref[0] + cells
            at = jnp.where(at < 0, at + total, at)
            row.append(jnp.where(at >= total, at - total, at))
        table.append(row)
    return table


def combined_channel(masks, h, p):
    cells = p.shape[0]
    slots = len(masks[0])
    users = h.shape[0] // (slots * cells)
    half = p.shape[-1] // 2
    wide = p.astype(F32)
    lane = lax.broadcasted_iota(jnp.int32, wide.shape[1:], 1)
    p0 = [jnp.where(lane < half, wide[n], -wide[n]) for n in range(cells)]
    p1 = [pltpu.roll(wide[n], half, 1) for n in range(cells)]
    rows = [r for n in range(cells) for r in (p0[n], -p1[n])] + [r for n in range(cells) for r in (p1[n], p0[n])]
    rhs = jnp.concatenate(rows, axis=0).astype(BF16)
    prod = lax.dot_general(h, rhs, NT, preferred_element_type=F32)
    width = prod.shape[1] // 2
    out = []
    for z in range(2):
        for c in range(cells):
            acc = jnp.zeros((users, width), F32)
            for k in range(slots):
                start = (k * cells + c) * users
                part = prod[start : start + users, z * width : (z + 1) * width]
                acc = jnp.where(masks[c][k], part, acc)
            out.append(acc)
    return jnp.concatenate(out, axis=0).astype(BF16)


def source_masks(table, base, users, cells, width):
    source = lax.broadcasted_iota(jnp.int32, (users, width), 1) // (width // cells) + base
    return [[source == at for at in row] for row in table]


def pick_subbands(res, per):
    rows = res.shape[0] // per
    lane = lax.broadcasted_iota(jnp.int32, (rows, LANES), 1) // (LANES // per)
    out = res[:rows]
    for i in range(1, per):
        out = jnp.where(lane == i, res[i * rows : (i + 1) * rows], out)
    return out


def own_kernel(total, chunks, near_ref, base_ref, h_ref, own_ref, p_ref, *refs):
    s_refs, acc_refs = refs[: len(chunks)], refs[len(chunks) :]
    blocks = max(first + count for _, first, count in chunks)
    subbands, cells = p_ref.shape[1], p_ref.shape[0]
    per = subbands // blocks
    users = own_ref.shape[1] // cells
    table = place(near_ref, base_ref, total, cells, h_ref.shape[1] // (cells * users))
    table = [row + [cells + c] for c, row in enumerate(table)]
    masks = source_masks(table, cells, users, cells, s_refs[0].shape[0])
    for r in range(blocks):
        g = []
        for b in range(r * per, (r + 1) * per):
            h = jnp.concatenate([h_ref[b], own_ref[b]], axis=0)
            g.append(combined_channel(masks, h, p_ref[:, b]))
        g = jnp.concatenate(g, axis=0)
        for s_ref, acc_ref, (_, first, count) in zip(s_refs, acc_refs, chunks):
            if first <= r < first + count:
                at = r - first
                res = jnp.dot(g, s_ref[:, at * LANES : (at + 1) * LANES], preferred_element_type=F32)
                acc_ref[at] = pick_subbands(res, per)


def remote_kernel(total, users, near_ref, base_ref, h_ref, a_ref, b_ref, g_ref):
    subbands, cells = a_ref.shape[1], a_ref.shape[0]
    blocks = g_ref.shape[0]
    per = subbands // blocks
    width = g_ref.shape[2] // 2
    rows = 2 * cells * users
    table = place(near_ref, base_ref, total, cells, h_ref.shape[1] // (cells * users))
    for side, (ref, base) in enumerate(((a_ref, 0), (b_ref, 2 * cells))):
        masks = source_masks(table, base, users, cells, width)
        for b in range(subbands):
            r, i = divmod(b, per)
            g_ref[r, i * rows : (i + 1) * rows, side * width : (side + 1) * width] = combined_channel(
                masks, h_ref[b], ref[:, b]
            )


def grid_kernel(chunk, me_ref, g_ref, a_ref, b_ref, acc_ref, noise_ref, *refs):
    outs, y, turned, tiles = refs[:-3], refs[-3], refs[-2], refs[-1]
    t, start, _ = chunk
    blocks, rows, _ = acc_ref.shape
    per = g_ref.shape[1] // rows
    _, users = noise_ref.shape[:2]
    for r in range(blocks):
        lanes = slice(r * LANES, (r + 1) * LANES)
        s = jnp.concatenate([a_ref[:, lanes], b_ref[:, lanes]], axis=0)
        res = jnp.dot(g_ref[start + r], s, preferred_element_type=F32)
        y[r * rows : (r + 1) * rows] = acc_ref[r] + pick_subbands(res, per)
    half = rows // 2
    step = 8
    for first in range(0, half, step):
        for part in range(2 * blocks // step):
            src = [divmod(part * step + i, 2) for i in range(step)]
            group = [y[r * rows + z * half + first : r * rows + z * half + first + step] for r, z in src]
            turned[part, first : first + step] = jnp.swapaxes(jnp.stack(group), 0, 1)
    for row in range(half):
        c, u = divmod(row, users)
        tile = jnp.concatenate([turned[part, row] for part in range(2 * blocks // step)], axis=0)
        tiles[u, c] = (tile + noise_ref[c, u, t, 2 * start : 2 * (start + blocks)].astype(F32)).astype(BF16)
    count = len(outs)
    for d in range(count):
        group = partner(me_ref[0], d, count)
        outs[d][...] = tiles[pl.ds(group * (users // count), users // count)]


def swap_groups(parts, width):
    parts = list(parts)
    lane = lax.broadcasted_iota(jnp.int32, parts[0].shape, 1)
    step = len(parts) // 2
    while step:
        low = (lane // (width * step)) % 2 == 0
        for i in range(len(parts)):
            if i & step == 0:
                x, y = parts[i], parts[i + step]
                parts[i] = jnp.where(low, x, pltpu.roll(y, width * step, 1))
                parts[i + step] = jnp.where(low, pltpu.roll(x, LANES - width * step, 1), y)
        step //= 2
    return parts


def time_kernel(t, halves, w1_ref, tw_ref, w2_ref, *refs):
    out_ref, held, sems = refs[-3:]
    rows = tw_ref.shape[1]
    share, cells, tall, _ = refs[0].shape
    parts = refs[: 2 * rows // tall]
    seqs = share * cells
    per = LANES // rows
    w1 = w1_ref[...]
    w2 = w2_ref[...]
    tall = w2.shape[0] // per
    batch = min(seqs, 2 * per)
    held_as = BF16 if halves == 1 else F32
    copies = []
    for first in range(0, seqs, batch):
        data = [
            jnp.concatenate([p[q // cells, q % cells].astype(held_as) for p in parts], axis=0)
            for q in range(first, first + batch)
        ]
        data = jnp.concatenate(data, axis=1).astype(BF16)
        both = jnp.dot(w1, data, preferred_element_type=F32)
        turned = []
        for q in range(batch):
            re = both[:rows, q * LANES : (q + 1) * LANES]
            im = both[rows:, q * LANES : (q + 1) * LANES]
            turned.append(
                jnp.concatenate([re * tw_ref[0] - im * tw_ref[1], re * tw_ref[1] + im * tw_ref[0]], axis=1)
            )
        turned = jnp.concatenate(turned, axis=0)
        prod = lax.dot_general(w2, turned.astype(BF16), NT, preferred_element_type=F32)
        for quad in range(batch // per):
            lanes = slice(quad * LANES, (quad + 1) * LANES)
            pieces = swap_groups([prod[i * tall : (i + 1) * tall, lanes].astype(BF16) for i in range(per)], rows)
            for at, piece in enumerate(pieces):
                u, c = divmod(first + quad * per + at, cells)
                held[u, c] = piece
                if c == cells - 1:
                    copies.append(pltpu.make_async_copy(held.at[u], out_ref.at[:, u, t], sems.at[u]))
                    copies[-1].start()
    for copy in copies:
        copy.wait()


def rotation(angle):
    return np.block([[np.cos(angle), -np.sin(angle)], [np.sin(angle), np.cos(angle)]])


def tables(length, parts):
    rows = length // LANES
    local = rows // parts
    m = np.arange(rows)
    w1 = []
    for me in range(parts):
        source = [(me - d) % parts for d in range(parts)]
        order = np.concatenate([src * local + np.arange(local) for src in source])
        angle = 2 * np.pi * (np.outer(m, order) % rows) / rows
        full = rotation(angle).reshape(2 * rows, 2, rows).transpose(0, 2, 1).reshape(2 * rows, 2 * rows)
        w1.append(full.astype(jnp.bfloat16))
    lane = np.arange(LANES)
    angle = 2 * np.pi * (np.outer(m, lane) % length) / length
    twist = (np.stack([np.cos(angle), np.sin(angle)]) / math.sqrt(length)).astype(np.float32)
    per = LANES // rows
    angle = 2 * np.pi * (np.outer(lane, lane) % LANES) / LANES
    w2 = rotation(angle).reshape(2, rows, per, 2 * LANES).transpose(2, 1, 0, 3).reshape(2 * LANES, 2 * LANES)
    return np.stack(w1), twist, w2.astype(jnp.bfloat16)


def body(symbols, precoders, plan, own_channel, cross_channel, neighbours, noise):
    cells, times, streams, width = symbols.shape
    subbands, users, slots, ants = precoders.shape[1], own_channel.shape[1], cross_channel.shape[2], precoders.shape[3]
    blocks = width // LANES
    per = subbands // blocks
    parts = lax.axis_size("sc")
    ring = lax.axis_size("cell")
    length = width * parts
    rows = 2 * cells * users
    up = [(i, (i + 1) % ring) for i in range(ring)]
    down = [(j, i) for i, j in up]

    def both_ways(x):
        moved = []
        for pairs in (up, down):
            moved.append(lax.ppermute(x, "cell", pairs))
        return moved

    total = cells * ring
    tall = cells * streams
    vmem = pl.BlockSpec(memory_space=pltpu.MemorySpace.VMEM)
    smem = pl.BlockSpec(memory_space=SMEM)
    hbm = pl.BlockSpec(memory_space=pltpu.MemorySpace.HBM)

    def call(kernel, out_shape, ins, scalars, scratch=(), grant=16, flops=1_000_000_000, **more):
        return pl.pallas_call(
            kernel,
            in_specs=[smem] * scalars + [vmem] * (len(ins) - scalars),
            out_specs=jax.tree.map(lambda _: vmem, out_shape),
            out_shape=out_shape,
            scratch_shapes=scratch,
            compiler_params=pltpu.CompilerParams(vmem_limit_bytes=grant << 20),
            cost_estimate=pl.CostEstimate(flops=flops, bytes_accessed=4_000_000, transcendentals=0),
        )(*ins)

    p_before, p_after = both_ways(precoders)
    chunks = [(t, 0, blocks) for t in range(times - 1)]
    cut = blocks // 2
    chunks += [(times - 1, 0, cut), (times - 1, cut, blocks - cut)]
    gated = call(
        functools.partial(gate_kernel, chunks),
        [jax.ShapeDtypeStruct((tall, count * LANES), BF16) for _, _, count in chunks], (plan, symbols), 1,
    )
    halos = [both_ways(g) for g in gated]

    base = (lax.axis_index("cell") * cells).astype(jnp.int32)[None]
    me = lax.axis_index("sc").astype(jnp.int32)[None]
    cross = cross_channel.transpose(3, 2, 0, 1, 4).reshape(subbands, slots * cells * users, ants)
    own = own_channel.transpose(2, 0, 1, 3).reshape(subbands, cells * users, ants)
    noise_tiles = noise.reshape(cells, users, times, 2, blocks, LANES).transpose(0, 1, 2, 4, 3, 5)
    noise_tiles = noise_tiles.reshape(cells, users, times, 2 * blocks, LANES)

    acc = call(
        functools.partial(own_kernel, total, chunks),
        [jax.ShapeDtypeStruct((count, rows, LANES), F32) for _, _, count in chunks],
        (neighbours, base, cross, own, precoders, *gated), 2,
    )
    comb = call(
        functools.partial(remote_kernel, total, users),
        jax.ShapeDtypeStruct((blocks, per * rows, 2 * tall), BF16),
        (neighbours, base, cross, p_before, p_after), 2,
    )

    w1, twist, w2 = (jnp.asarray(x) for x in tables(length, parts))
    w1 = lax.dynamic_index_in_dim(w1, me[0], 0, False)
    share = users // parts
    full = (cells, share, times, 2 * length // LANES, LANES)
    out, got = None, []
    for at, (chunk, halo) in enumerate(zip(chunks, halos)):
        t, _, count = chunk
        tile = (share, cells, 2 * count, LANES)
        sent = call(
            functools.partial(grid_kernel, chunk), [jax.ShapeDtypeStruct(tile, BF16)] * parts,
            (me, comb, *halo, acc[at], noise_tiles), 1,
            scratch=[
                pltpu.VMEM((count * rows, LANES), F32),
                pltpu.VMEM((2 * count // 8, rows // 2, 8, LANES), F32),
                pltpu.VMEM((users, cells, 2 * count, LANES), BF16),
            ],
        )
        moved = {d: lax.ppermute(sent[d], "sc", [(i, (i ^ d) if ([0, 0, 0])[at] else (i + d) % parts) for i in range(parts)]) for d in ([(3,2,1),(3,2,1),(2,1,3)])[at]}
        got.append([sent[0]] + [moved[d] for d in range(1, parts)])
        if at + 1 < len(chunks) and chunks[at + 1][0] == t:
            continue
        halves = len(got)
        arrived = [got[h][d] for d in range(parts) for h in range(halves)]
        got = []
        ins = (w1, twist, w2, *arrived) + (() if out is None else (out,))
        out = pl.pallas_call(
            functools.partial(time_kernel, t, halves),
            in_specs=[vmem] * (3 + len(arrived)) + [hbm] * (t > 0),
            out_specs=hbm,
            out_shape=jax.ShapeDtypeStruct(full, BF16),
            input_output_aliases={3 + len(arrived): 0} if t else {},
            scratch_shapes=[
                pltpu.VMEM((share, cells, 2 * length // LANES, LANES), BF16),
                pltpu.SemaphoreType.DMA((share,)),
            ],
            name="time",
            compiler_params=pltpu.CompilerParams(vmem_limit_bytes=16 << 20),
            cost_estimate=pl.CostEstimate(flops=1_000_000_000, bytes_accessed=2_000_000, transcendentals=0),
        )(*ins)
    out = out.reshape(cells, share, times, length // LANES, 2, LANES).transpose(0, 1, 2, 4, 3, 5)
    return out.reshape(cells, share, times, 2, length)


def solution(mesh):
    in_specs = (
        P(("groups", "cell"), None, None, "sc"),
        P(("groups", "cell"), "sc", None, None),
        P(("groups", "cell")),
        P(("groups", "cell"), None, "sc", None),
        P(("groups", "cell"), None, None, "sc", None),
        P(("groups", "cell"), None),
        P(("groups", "cell"), None, None, None, "sc"),
    )
    out_specs = P(("groups", "cell"), "sc", None, None, None)
    return jax.shard_map(body, mesh=mesh, in_specs=in_specs, out_specs=out_specs, check_vma=False)
```

```python
import functools
import math

import jax
import jax.numpy as jnp
import numpy as np
from jax import lax
from jax.experimental import pallas as pl
from jax.experimental.pallas import tpu as pltpu
from jax.sharding import PartitionSpec as P


LANES = 128
SMEM = pltpu.MemorySpace.SMEM
BF16, F32 = jnp.bfloat16, jnp.float32
NT = (((1,), (1,)), ((), ()))


def partner(me, d, parts):
    return (me + d) % parts


def gate_kernel(chunks, plan_ref, x_ref, *outs):
    cells, _, streams, _ = x_ref.shape
    for c in range(cells):
        on = plan_ref[c] != 0
        for out, (t, first, count) in zip(outs, chunks):
            x = x_ref[c, t, :, first * LANES : (first + count) * LANES]
            out[c * streams : (c + 1) * streams] = jnp.where(on, x, jnp.zeros_like(x))


def place(near_ref, base_ref, total, cells, slots):
    table = []
    for c in range(cells):
        row = []
        for k in range(slots):
            at = near_ref[c, k] - base_ref[0] + cells
            at = jnp.where(at < 0, at + total, at)
            row.append(jnp.where(at >= total, at - total, at))
        table.append(row)
    return table


def combined_channel(masks, h, p):
    cells = p.shape[0]
    slots = len(masks[0])
    users = h.shape[0] // (slots * cells)
    half = p.shape[-1] // 2
    wide = p.astype(F32)
    lane = lax.broadcasted_iota(jnp.int32, wide.shape[1:], 1)
    p0 = [jnp.where(lane < half, wide[n], -wide[n]) for n in range(cells)]
    p1 = [pltpu.roll(wide[n], half, 1) for n in range(cells)]
    rows = [r for n in range(cells) for r in (p0[n], -p1[n])] + [r for n in range(cells) for r in (p1[n], p0[n])]
    rhs = jnp.concatenate(rows, axis=0).astype(BF16)
    prod = lax.dot_general(h, rhs, NT, preferred_element_type=F32)
    width = prod.shape[1] // 2
    out = []
    for z in range(2):
        for c in range(cells):
            acc = jnp.zeros((users, width), F32)
            for k in range(slots):
                start = (k * cells + c) * users
                part = prod[start : start + users, z * width : (z + 1) * width]
                acc = jnp.where(masks[c][k], part, acc)
            out.append(acc)
    return jnp.concatenate(out, axis=0).astype(BF16)


def source_masks(table, base, users, cells, width):
    source = lax.broadcasted_iota(jnp.int32, (users, width), 1) // (width // cells) + base
    return [[source == at for at in row] for row in table]


def pick_subbands(res, per):
    rows = res.shape[0] // per
    lane = lax.broadcasted_iota(jnp.int32, (rows, LANES), 1) // (LANES // per)
    out = res[:rows]
    for i in range(1, per):
        out = jnp.where(lane == i, res[i * rows : (i + 1) * rows], out)
    return out


def own_kernel(total, chunks, near_ref, base_ref, h_ref, own_ref, p_ref, *refs):
    s_refs, acc_refs = refs[: len(chunks)], refs[len(chunks) :]
    blocks = max(first + count for _, first, count in chunks)
    subbands, cells = p_ref.shape[1], p_ref.shape[0]
    per = subbands // blocks
    users = own_ref.shape[1] // cells
    table = place(near_ref, base_ref, total, cells, h_ref.shape[1] // (cells * users))
    table = [row + [cells + c] for c, row in enumerate(table)]
    masks = source_masks(table, cells, users, cells, s_refs[0].shape[0])
    for r in range(blocks):
        g = []
        for b in range(r * per, (r + 1) * per):
            h = jnp.concatenate([h_ref[b], own_ref[b]], axis=0)
            g.append(combined_channel(masks, h, p_ref[:, b]))
        g = jnp.concatenate(g, axis=0)
        for s_ref, acc_ref, (_, first, count) in zip(s_refs, acc_refs, chunks):
            if first <= r < first + count:
                at = r - first
                res = jnp.dot(g, s_ref[:, at * LANES : (at + 1) * LANES], preferred_element_type=F32)
                acc_ref[at] = pick_subbands(res, per)


def remote_kernel(total, users, near_ref, base_ref, h_ref, a_ref, b_ref, g_ref):
    subbands, cells = a_ref.shape[1], a_ref.shape[0]
    blocks = g_ref.shape[0]
    per = subbands // blocks
    width = g_ref.shape[2] // 2
    rows = 2 * cells * users
    table = place(near_ref, base_ref, total, cells, h_ref.shape[1] // (cells * users))
    for side, (ref, base) in enumerate(((a_ref, 0), (b_ref, 2 * cells))):
        masks = source_masks(table, base, users, cells, width)
        for b in range(subbands):
            r, i = divmod(b, per)
            g_ref[r, i * rows : (i + 1) * rows, side * width : (side + 1) * width] = combined_channel(
                masks, h_ref[b], ref[:, b]
            )


def grid_kernel(chunk, me_ref, g_ref, a_ref, b_ref, acc_ref, noise_ref, *refs):
    outs, y, turned, tiles = refs[:-3], refs[-3], refs[-2], refs[-1]
    t, start, _ = chunk
    blocks, rows, _ = acc_ref.shape
    per = g_ref.shape[1] // rows
    _, users = noise_ref.shape[:2]
    for r in range(blocks):
        lanes = slice(r * LANES, (r + 1) * LANES)
        s = jnp.concatenate([a_ref[:, lanes], b_ref[:, lanes]], axis=0)
        res = jnp.dot(g_ref[start + r], s, preferred_element_type=F32)
        y[r * rows : (r + 1) * rows] = acc_ref[r] + pick_subbands(res, per)
    half = rows // 2
    step = 8
    for first in range(0, half, step):
        for part in range(2 * blocks // step):
            src = [divmod(part * step + i, 2) for i in range(step)]
            group = [y[r * rows + z * half + first : r * rows + z * half + first + step] for r, z in src]
            turned[part, first : first + step] = jnp.swapaxes(jnp.stack(group), 0, 1)
    for row in range(half):
        c, u = divmod(row, users)
        tile = jnp.concatenate([turned[part, row] for part in range(2 * blocks // step)], axis=0)
        tiles[u, c] = (tile + noise_ref[c, u, t, 2 * start : 2 * (start + blocks)].astype(F32)).astype(BF16)
    count = len(outs)
    for d in range(count):
        group = partner(me_ref[0], d, count)
        outs[d][...] = tiles[pl.ds(group * (users // count), users // count)]


def swap_groups(parts, width):
    parts = list(parts)
    lane = lax.broadcasted_iota(jnp.int32, parts[0].shape, 1)
    step = len(parts) // 2
    while step:
        low = (lane // (width * step)) % 2 == 0
        for i in range(len(parts)):
            if i & step == 0:
                x, y = parts[i], parts[i + step]
                parts[i] = jnp.where(low, x, pltpu.roll(y, width * step, 1))
                parts[i + step] = jnp.where(low, pltpu.roll(x, LANES - width * step, 1), y)
        step //= 2
    return parts


def time_kernel(t, halves, w1_ref, tw_ref, w2_ref, *refs):
    out_ref, held, sems = refs[-3:]
    rows = tw_ref.shape[1]
    share, cells, tall, _ = refs[0].shape
    parts = refs[: 2 * rows // tall]
    seqs = share * cells
    per = LANES // rows
    w1 = w1_ref[...]
    w2 = w2_ref[...]
    n2 = w2.shape[0] // 2
    tall = n2 // per
    batch = min(seqs, 2 * per)
    held_as = BF16 if halves == 1 else F32
    copies = []
    for first in range(0, seqs, batch):
        data = [
            jnp.concatenate([p[q // cells, q % cells].astype(held_as) for p in parts], axis=0)
            for q in range(first, first + batch)
        ]
        data = jnp.concatenate(data, axis=1).astype(BF16)
        both = jnp.dot(w1, data, preferred_element_type=F32)
        both = both[: 2 * rows] + both[2 * rows :]
        turned = []
        for q in range(batch):
            re = both[:rows, q * LANES : (q + 1) * LANES]
            im = both[rows:, q * LANES : (q + 1) * LANES]
            turned.append(
                jnp.concatenate([re * tw_ref[0] - im * tw_ref[1], re * tw_ref[1] + im * tw_ref[0]], axis=1)
            )
        turned = jnp.concatenate(turned, axis=0)
        high = turned.astype(BF16)
        low = (turned - high.astype(F32)).astype(BF16)
        prod = lax.dot_general(w2, high, NT, preferred_element_type=F32)
        prod = prod[:n2] + prod[n2:] + lax.dot_general(w2[:n2], low, NT, preferred_element_type=F32)
        for quad in range(batch // per):
            lanes = slice(quad * LANES, (quad + 1) * LANES)
            pieces = swap_groups([prod[i * tall : (i + 1) * tall, lanes].astype(BF16) for i in range(per)], rows)
            for at, piece in enumerate(pieces):
                u, c = divmod(first + quad * per + at, cells)
                held[u, c] = piece
                if c == cells - 1:
                    copies.append(pltpu.make_async_copy(held.at[u], out_ref.at[:, u, t], sems.at[u]))
                    copies[-1].start()
    for copy in copies:
        copy.wait()


def rotation(angle):
    return np.block([[np.cos(angle), -np.sin(angle)], [np.sin(angle), np.cos(angle)]])


def split_rows(table):
    high = table.astype(jnp.bfloat16)
    low = (table - high.astype(np.float64)).astype(jnp.bfloat16)
    return np.concatenate([high, low], axis=0)


def tables(length, parts):
    rows = length // LANES
    local = rows // parts
    m = np.arange(rows)
    w1 = []
    for me in range(parts):
        source = [(me - d) % parts for d in range(parts)]
        order = np.concatenate([src * local + np.arange(local) for src in source])
        angle = 2 * np.pi * (np.outer(m, order) % rows) / rows
        full = rotation(angle).reshape(2 * rows, 2, rows).transpose(0, 2, 1).reshape(2 * rows, 2 * rows)
        w1.append(split_rows(full))
    lane = np.arange(LANES)
    angle = 2 * np.pi * (np.outer(m, lane) % length) / length
    twist = (np.stack([np.cos(angle), np.sin(angle)]) / math.sqrt(length)).astype(np.float32)
    per = LANES // rows
    angle = 2 * np.pi * (np.outer(lane, lane) % LANES) / LANES
    w2 = rotation(angle).reshape(2, rows, per, 2 * LANES).transpose(2, 1, 0, 3).reshape(2 * LANES, 2 * LANES)
    return np.stack(w1), twist, split_rows(w2)


def body(symbols, precoders, plan, own_channel, cross_channel, neighbours, noise):
    cells, times, streams, width = symbols.shape
    subbands, users, slots, ants = precoders.shape[1], own_channel.shape[1], cross_channel.shape[2], precoders.shape[3]
    blocks = width // LANES
    per = subbands // blocks
    parts = lax.axis_size("sc")
    ring = lax.axis_size("cell")
    length = width * parts
    rows = 2 * cells * users
    up = [(i, (i + 1) % ring) for i in range(ring)]
    down = [(j, i) for i, j in up]

    def both_ways(x):
        moved = []
        for pairs in (up, down):
            moved.append(lax.ppermute(x, "cell", pairs))
        return moved

    total = cells * ring
    tall = cells * streams
    vmem = pl.BlockSpec(memory_space=pltpu.MemorySpace.VMEM)
    smem = pl.BlockSpec(memory_space=SMEM)
    hbm = pl.BlockSpec(memory_space=pltpu.MemorySpace.HBM)

    def call(kernel, out_shape, ins, scalars, scratch=(), grant=16, flops=1_000_000_000, **more):
        return pl.pallas_call(
            kernel,
            in_specs=[smem] * scalars + [vmem] * (len(ins) - scalars),
            out_specs=jax.tree.map(lambda _: vmem, out_shape),
            out_shape=out_shape,
            scratch_shapes=scratch,
            compiler_params=pltpu.CompilerParams(vmem_limit_bytes=grant << 20),
            cost_estimate=pl.CostEstimate(flops=flops, bytes_accessed=4_000_000, transcendentals=0),
        )(*ins)

    p_before, p_after = both_ways(precoders)
    base = (lax.axis_index("cell") * cells).astype(jnp.int32)[None]
    me = lax.axis_index("sc").astype(jnp.int32)[None]
    w1, twist, w2 = (jnp.asarray(x) for x in tables(length, parts))
    w1 = lax.dynamic_index_in_dim(w1, me[0], 0, False)
    plan, base, me, w1 = lax.optimization_barrier((plan, base, me, w1))
    chunks = [(t, 0, blocks) for t in range(times - 1)]
    cut = blocks // 2
    chunks += [(times - 1, 0, cut), (times - 1, cut, blocks - cut)]
    gated = call(
        functools.partial(gate_kernel, chunks),
        [jax.ShapeDtypeStruct((tall, count * LANES), BF16) for _, _, count in chunks], (plan, symbols), 1,
    )
    halos = [both_ways(g) for g in gated]

    cross = cross_channel.transpose(3, 2, 0, 1, 4).reshape(subbands, slots * cells * users, ants)
    own = own_channel.transpose(2, 0, 1, 3).reshape(subbands, cells * users, ants)
    noise_tiles = noise.reshape(cells, users, times, 2, blocks, LANES).transpose(0, 1, 2, 4, 3, 5)
    noise_tiles = noise_tiles.reshape(cells, users, times, 2 * blocks, LANES)

    acc = call(
        functools.partial(own_kernel, total, chunks),
        [jax.ShapeDtypeStruct((count, rows, LANES), F32) for _, _, count in chunks],
        (neighbours, base, cross, own, precoders, *gated), 2,
    )
    comb = call(
        functools.partial(remote_kernel, total, users),
        jax.ShapeDtypeStruct((blocks, per * rows, 2 * tall), BF16),
        (neighbours, base, cross, p_before, p_after), 2,
    )

    share = users // parts
    full = (cells, share, times, 2 * length // LANES, LANES)
    out, got = None, []
    for at, (chunk, halo) in enumerate(zip(chunks, halos)):
        t, _, count = chunk
        tile = (share, cells, 2 * count, LANES)
        sent = call(
            functools.partial(grid_kernel, chunk), [jax.ShapeDtypeStruct(tile, BF16)] * parts,
            (me, comb, *halo, acc[at], noise_tiles), 1,
            scratch=[
                pltpu.VMEM((count * rows, LANES), F32),
                pltpu.VMEM((2 * count // 8, rows // 2, 8, LANES), F32),
                pltpu.VMEM((users, cells, 2 * count, LANES), BF16),
            ],
        )
        moved = {}
        for d in range(1, parts):
            moved[d] = lax.ppermute(sent[d], "sc", [(i, (i + d) % parts) for i in range(parts)])
        got.append([sent[0]] + [moved[d] for d in range(1, parts)])
        if at + 1 < len(chunks) and chunks[at + 1][0] == t:
            continue
        halves = len(got)
        arrived = [got[h][d] for d in range(parts) for h in range(halves)]
        got = []
        ins = (w1, twist, w2, *arrived) + (() if out is None else (out,))
        out = pl.pallas_call(
            functools.partial(time_kernel, t, halves),
            in_specs=[vmem] * (3 + len(arrived)) + [hbm] * (t > 0),
            out_specs=hbm,
            out_shape=jax.ShapeDtypeStruct(full, BF16),
            input_output_aliases={3 + len(arrived): 0} if t else {},
            scratch_shapes=[
                pltpu.VMEM((share, cells, 2 * length // LANES, LANES), BF16),
                pltpu.SemaphoreType.DMA((share,)),
            ],
            name="time",
            compiler_params=pltpu.CompilerParams(vmem_limit_bytes=16 << 20),
            cost_estimate=pl.CostEstimate(flops=1_000_000_000, bytes_accessed=2_000_000, transcendentals=0),
        )(*ins)
    out = out.reshape(cells, share, times, length // LANES, 2, LANES).transpose(0, 1, 2, 4, 3, 5)
    return out.reshape(cells, share, times, 2, length)


def solution(mesh):
    in_specs = (
        P(("groups", "cell"), None, None, "sc"),
        P(("groups", "cell"), "sc", None, None),
        P(("groups", "cell")),
        P(("groups", "cell"), None, "sc", None),
        P(("groups", "cell"), None, None, "sc", None),
        P(("groups", "cell"), None),
        P(("groups", "cell"), None, None, None, "sc"),
    )
    out_specs = P(("groups", "cell"), "sc", None, None, None)
    return jax.shard_map(body, mesh=mesh, in_specs=in_specs, out_specs=out_specs, check_vma=False)
```

```python
import functools
import math

import jax
import jax.numpy as jnp
import numpy as np
from jax import lax
from jax.experimental import pallas as pl
from jax.experimental.pallas import tpu as pltpu
from jax.sharding import PartitionSpec as P


LANES = 128
SMEM = pltpu.MemorySpace.SMEM
BF16, F32 = jnp.bfloat16, jnp.float32
NT = (((1,), (1,)), ((), ()))


def partner(me, d, parts):
    return (me + d) % parts


def gate_kernel(chunks, plan_ref, x_ref, *outs):
    cells, _, streams, _ = x_ref.shape
    for c in range(cells):
        on = plan_ref[c] != 0
        for out, (t, first, count) in zip(outs, chunks):
            x = x_ref[c, t, :, first * LANES : (first + count) * LANES]
            out[c * streams : (c + 1) * streams] = jnp.where(on, x, jnp.zeros_like(x))


def place(near_ref, base_ref, total, cells, slots):
    table = []
    for c in range(cells):
        row = []
        for k in range(slots):
            at = near_ref[c, k] - base_ref[0] + cells
            at = jnp.where(at < 0, at + total, at)
            row.append(jnp.where(at >= total, at - total, at))
        table.append(row)
    return table


def combined_channel(masks, h, p):
    cells = p.shape[0]
    slots = len(masks[0])
    users = h.shape[0] // (slots * cells)
    half = p.shape[-1] // 2
    wide = p.astype(F32)
    lane = lax.broadcasted_iota(jnp.int32, wide.shape[1:], 1)
    p0 = [jnp.where(lane < half, wide[n], -wide[n]) for n in range(cells)]
    p1 = [pltpu.roll(wide[n], half, 1) for n in range(cells)]
    rows = [r for n in range(cells) for r in (p0[n], -p1[n])] + [r for n in range(cells) for r in (p1[n], p0[n])]
    rhs = jnp.concatenate(rows, axis=0).astype(BF16)
    prod = lax.dot_general(h, rhs, NT, preferred_element_type=F32)
    width = prod.shape[1] // 2
    out = []
    for z in range(2):
        for c in range(cells):
            acc = jnp.zeros((users, width), F32)
            for k in range(slots):
                start = (k * cells + c) * users
                part = prod[start : start + users, z * width : (z + 1) * width]
                acc = jnp.where(masks[c][k], part, acc)
            out.append(acc)
    return jnp.concatenate(out, axis=0).astype(BF16)


def source_masks(table, base, users, cells, width):
    source = lax.broadcasted_iota(jnp.int32, (users, width), 1) // (width // cells) + base
    return [[source == at for at in row] for row in table]


def pick_subbands(res, per):
    rows = res.shape[0] // per
    lane = lax.broadcasted_iota(jnp.int32, (rows, LANES), 1) // (LANES // per)
    out = res[:rows]
    for i in range(1, per):
        out = jnp.where(lane == i, res[i * rows : (i + 1) * rows], out)
    return out


def own_kernel(total, chunks, near_ref, base_ref, h_ref, own_ref, p_ref, *refs):
    s_refs, acc_refs = refs[: len(chunks)], refs[len(chunks) :]
    blocks = max(first + count for _, first, count in chunks)
    subbands, cells = p_ref.shape[1], p_ref.shape[0]
    per = subbands // blocks
    users = own_ref.shape[1] // cells
    table = place(near_ref, base_ref, total, cells, h_ref.shape[1] // (cells * users))
    table = [row + [cells + c] for c, row in enumerate(table)]
    masks = source_masks(table, cells, users, cells, s_refs[0].shape[0])
    for r in range(blocks):
        g = []
        for b in range(r * per, (r + 1) * per):
            h = jnp.concatenate([h_ref[b], own_ref[b]], axis=0)
            g.append(combined_channel(masks, h, p_ref[:, b]))
        g = jnp.concatenate(g, axis=0)
        for s_ref, acc_ref, (_, first, count) in zip(s_refs, acc_refs, chunks):
            if first <= r < first + count:
                at = r - first
                res = jnp.dot(g, s_ref[:, at * LANES : (at + 1) * LANES], preferred_element_type=F32)
                acc_ref[at] = pick_subbands(res, per)


def remote_kernel(total, users, near_ref, base_ref, h_ref, a_ref, b_ref, g_ref):
    subbands, cells = a_ref.shape[1], a_ref.shape[0]
    blocks = g_ref.shape[0]
    per = subbands // blocks
    width = g_ref.shape[2] // 2
    rows = 2 * cells * users
    table = place(near_ref, base_ref, total, cells, h_ref.shape[1] // (cells * users))
    for side, (ref, base) in enumerate(((a_ref, 0), (b_ref, 2 * cells))):
        masks = source_masks(table, base, users, cells, width)
        for b in range(subbands):
            r, i = divmod(b, per)
            g_ref[r, i * rows : (i + 1) * rows, side * width : (side + 1) * width] = combined_channel(
                masks, h_ref[b], ref[:, b]
            )


def grid_kernel(chunk, me_ref, g_ref, a_ref, b_ref, acc_ref, noise_ref, *refs):
    outs, y, turned, tiles = refs[:-3], refs[-3], refs[-2], refs[-1]
    t, start, _ = chunk
    blocks, rows, _ = acc_ref.shape
    per = g_ref.shape[1] // rows
    _, users = noise_ref.shape[:2]
    for r in range(blocks):
        lanes = slice(r * LANES, (r + 1) * LANES)
        s = jnp.concatenate([a_ref[:, lanes], b_ref[:, lanes]], axis=0)
        res = jnp.dot(g_ref[start + r], s, preferred_element_type=F32)
        y[r * rows : (r + 1) * rows] = acc_ref[r] + pick_subbands(res, per)
    half = rows // 2
    step = 8
    for first in range(0, half, step):
        for part in range(2 * blocks // step):
            src = [divmod(part * step + i, 2) for i in range(step)]
            group = [y[r * rows + z * half + first : r * rows + z * half + first + step] for r, z in src]
            turned[part, first : first + step] = jnp.swapaxes(jnp.stack(group), 0, 1)
    for row in range(half):
        c, u = divmod(row, users)
        tile = jnp.concatenate([turned[part, row] for part in range(2 * blocks // step)], axis=0)
        tiles[u, c] = (tile + noise_ref[c, u, t, 2 * start : 2 * (start + blocks)].astype(F32)).astype(BF16)
    count = len(outs)
    for d in range(count):
        group = partner(me_ref[0], d, count)
        outs[d][...] = tiles[pl.ds(group * (users // count), users // count)]


def swap_groups(parts, width):
    parts = list(parts)
    lane = lax.broadcasted_iota(jnp.int32, parts[0].shape, 1)
    step = len(parts) // 2
    while step:
        low = (lane // (width * step)) % 2 == 0
        for i in range(len(parts)):
            if i & step == 0:
                x, y = parts[i], parts[i + step]
                parts[i] = jnp.where(low, x, pltpu.roll(y, width * step, 1))
                parts[i + step] = jnp.where(low, pltpu.roll(x, LANES - width * step, 1), y)
        step //= 2
    return parts


def time_kernel(t, halves, w1_ref, tw_ref, w2_ref, *refs):
    out_ref, held, sems = refs[-3:]
    rows = tw_ref.shape[1]
    share, cells, tall, _ = refs[0].shape
    parts = refs[: 2 * rows // tall]
    seqs = share * cells
    per = LANES // rows
    w1 = w1_ref[...]
    w2 = w2_ref[...]
    tall = w2.shape[0] // per
    batch = min(seqs, 2 * per)
    held_as = BF16 if halves == 1 else F32
    copies = []
    for first in range(0, seqs, batch):
        data = [
            jnp.concatenate([p[q // cells, q % cells].astype(held_as) for p in parts], axis=0)
            for q in range(first, first + batch)
        ]
        data = jnp.concatenate(data, axis=1).astype(BF16)
        both = jnp.dot(w1, data, preferred_element_type=F32)
        turned = []
        for q in range(batch):
            re = both[:rows, q * LANES : (q + 1) * LANES]
            im = both[rows:, q * LANES : (q + 1) * LANES]
            turned.append(
                jnp.concatenate([re * tw_ref[0] - im * tw_ref[1], re * tw_ref[1] + im * tw_ref[0]], axis=1)
            )
        turned = jnp.concatenate(turned, axis=0)
        prod = lax.dot_general(w2, turned.astype(BF16), NT, preferred_element_type=F32)
        for quad in range(batch // per):
            lanes = slice(quad * LANES, (quad + 1) * LANES)
            pieces = swap_groups([prod[i * tall : (i + 1) * tall, lanes].astype(BF16) for i in range(per)], rows)
            for at, piece in enumerate(pieces):
                u, c = divmod(first + quad * per + at, cells)
                held[u, c] = piece
                if c == cells - 1:
                    copies.append(pltpu.make_async_copy(held.at[u], out_ref.at[:, u, t], sems.at[u]))
                    copies[-1].start()
    for copy in copies:
        copy.wait()


def rotation(angle):
    return np.block([[np.cos(angle), -np.sin(angle)], [np.sin(angle), np.cos(angle)]])


def tables(length, parts):
    rows = length // LANES
    local = rows // parts
    m = np.arange(rows)
    w1 = []
    for me in range(parts):
        source = [(me - d) % parts for d in range(parts)]
        order = np.concatenate([src * local + np.arange(local) for src in source])
        angle = 2 * np.pi * (np.outer(m, order) % rows) / rows
        full = rotation(angle).reshape(2 * rows, 2, rows).transpose(0, 2, 1).reshape(2 * rows, 2 * rows)
        w1.append(full.astype(jnp.bfloat16))
    lane = np.arange(LANES)
    angle = 2 * np.pi * (np.outer(m, lane) % length) / length
    twist = (np.stack([np.cos(angle), np.sin(angle)]) / math.sqrt(length)).astype(np.float32)
    per = LANES // rows
    angle = 2 * np.pi * (np.outer(lane, lane) % LANES) / LANES
    w2 = rotation(angle).reshape(2, rows, per, 2 * LANES).transpose(2, 1, 0, 3).reshape(2 * LANES, 2 * LANES)
    return np.stack(w1), twist, w2.astype(jnp.bfloat16)


def body(symbols, precoders, plan, own_channel, cross_channel, neighbours, noise):
    cells, times, streams, width = symbols.shape
    subbands, users, slots, ants = precoders.shape[1], own_channel.shape[1], cross_channel.shape[2], precoders.shape[3]
    blocks = width // LANES
    per = subbands // blocks
    parts = lax.axis_size("sc")
    ring = lax.axis_size("cell")
    length = width * parts
    rows = 2 * cells * users
    up = [(i, (i + 1) % ring) for i in range(ring)]
    down = [(j, i) for i, j in up]

    def both_ways(x):
        moved = []
        for pairs in (up, down):
            moved.append(lax.ppermute(x, "cell", pairs))
        return moved

    total = cells * ring
    tall = cells * streams
    vmem = pl.BlockSpec(memory_space=pltpu.MemorySpace.VMEM)
    smem = pl.BlockSpec(memory_space=SMEM)
    hbm = pl.BlockSpec(memory_space=pltpu.MemorySpace.HBM)

    def call(kernel, out_shape, ins, scalars, scratch=(), grant=16, flops=1_000_000_000, **more):
        return pl.pallas_call(
            kernel,
            in_specs=[smem] * scalars + [vmem] * (len(ins) - scalars),
            out_specs=jax.tree.map(lambda _: vmem, out_shape),
            out_shape=out_shape,
            scratch_shapes=scratch,
            compiler_params=pltpu.CompilerParams(vmem_limit_bytes=grant << 20),
            cost_estimate=pl.CostEstimate(flops=flops, bytes_accessed=4_000_000, transcendentals=0),
        )(*ins)

    p_before, p_after = both_ways(precoders)
    base = (lax.axis_index("cell") * cells).astype(jnp.int32)[None]
    me = lax.axis_index("sc").astype(jnp.int32)[None]
    w1, twist, w2 = (jnp.asarray(x) for x in tables(length, parts))
    w1 = lax.dynamic_index_in_dim(w1, me[0], 0, False)
    plan, base, me, w1 = lax.optimization_barrier((plan, base, me, w1))
    chunks = [(t, 0, blocks) for t in range(times - 1)]
    cut = blocks // 2
    chunks += [(times - 1, 0, cut), (times - 1, cut, blocks - cut)]
    gated = call(
        functools.partial(gate_kernel, chunks),
        [jax.ShapeDtypeStruct((tall, count * LANES), BF16) for _, _, count in chunks], (plan, symbols), 1,
    )
    halos = [both_ways(g) for g in gated]

    cross = cross_channel.transpose(3, 2, 0, 1, 4).reshape(subbands, slots * cells * users, ants)
    own = own_channel.transpose(2, 0, 1, 3).reshape(subbands, cells * users, ants)
    noise_tiles = noise.reshape(cells, users, times, 2, blocks, LANES).transpose(0, 1, 2, 4, 3, 5)
    noise_tiles = noise_tiles.reshape(cells, users, times, 2 * blocks, LANES)

    acc = call(
        functools.partial(own_kernel, total, chunks),
        [jax.ShapeDtypeStruct((count, rows, LANES), F32) for _, _, count in chunks],
        (neighbours, base, cross, own, precoders, *gated), 2,
    )
    comb = call(
        functools.partial(remote_kernel, total, users),
        jax.ShapeDtypeStruct((blocks, per * rows, 2 * tall), BF16),
        (neighbours, base, cross, p_before, p_after), 2,
    )

    share = users // parts
    full = (cells, share, times, 2 * length // LANES, LANES)
    out, got = None, []
    for at, (chunk, halo) in enumerate(zip(chunks, halos)):
        t, _, count = chunk
        tile = (share, cells, 2 * count, LANES)
        sent = call(
            functools.partial(grid_kernel, chunk), [jax.ShapeDtypeStruct(tile, BF16)] * parts,
            (me, comb, *halo, acc[at], noise_tiles), 1,
            scratch=[
                pltpu.VMEM((count * rows, LANES), F32),
                pltpu.VMEM((2 * count // 8, rows // 2, 8, LANES), F32),
                pltpu.VMEM((users, cells, 2 * count, LANES), BF16),
            ],
        )
        moved = {}
        for d in range(1, parts):
            moved[d] = lax.ppermute(sent[d], "sc", [(i, (i + d) % parts) for i in range(parts)])
        got.append([sent[0]] + [moved[d] for d in range(1, parts)])
        if at + 1 < len(chunks) and chunks[at + 1][0] == t:
            continue
        halves = len(got)
        arrived = [got[h][d] for d in range(parts) for h in range(halves)]
        got = []
        ins = (w1, twist, w2, *arrived) + (() if out is None else (out,))
        out = pl.pallas_call(
            functools.partial(time_kernel, t, halves),
            in_specs=[vmem] * (3 + len(arrived)) + [hbm] * (t > 0),
            out_specs=hbm,
            out_shape=jax.ShapeDtypeStruct(full, BF16),
            input_output_aliases={3 + len(arrived): 0} if t else {},
            scratch_shapes=[
                pltpu.VMEM((share, cells, 2 * length // LANES, LANES), BF16),
                pltpu.SemaphoreType.DMA((share,)),
            ],
            name="time",
            compiler_params=pltpu.CompilerParams(vmem_limit_bytes=16 << 20),
            cost_estimate=pl.CostEstimate(flops=1_000_000_000, bytes_accessed=2_000_000, transcendentals=0),
        )(*ins)
    out = out.reshape(cells, share, times, length // LANES, 2, LANES).transpose(0, 1, 2, 4, 3, 5)
    return out.reshape(cells, share, times, 2, length)


def solution(mesh):
    in_specs = (
        P(("groups", "cell"), None, None, "sc"),
        P(("groups", "cell"), "sc", None, None),
        P(("groups", "cell")),
        P(("groups", "cell"), None, "sc", None),
        P(("groups", "cell"), None, None, "sc", None),
        P(("groups", "cell"), None),
        P(("groups", "cell"), None, None, None, "sc"),
    )
    out_specs = P(("groups", "cell"), "sc", None, None, None)
    return jax.shard_map(body, mesh=mesh, in_specs=in_specs, out_specs=out_specs, check_vma=False)
```
